32 devices in a mesh: shard: 8 (over z, x), head: 4 (over y, core).
Axes of the slice: x: 2, y: 2, z: 4, core: 2. Of those that a mesh axis runs over, the one named last changes fastest.
Arguments:
- resid_in: float32 [2048, 1024], P(('shard', 'head')), may hold values from -6 to 6
- cotangent: float32 [2048, 1024], P(('shard', 'head')), may hold values from -6 to 6
- segment: int32 [2048], P('shard'), may hold values from 0 to 3, never falling along the last dimension, each value on 1 to 1024 neighbouring positions
- attn_gain: bfloat16 [1024], P('shard'), may hold values from 0.25 to 1.75
- w_query: bfloat16 [1024, 512], P('shard', 'head'), may hold values from -0.1875 to 0.1875
- w_key: bfloat16 [1024, 512], P('shard', 'head'), may hold values from -0.1875 to 0.1875
- w_value: bfloat16 [1024, 1024], P('shard', 'head'), may hold values from -0.1875 to 0.1875
- w_outgate: bfloat16 [1024, 1024], P('shard', 'head'), may hold values from -0.1875 to 0.1875
- w_low: bfloat16 [1024, 16], P('shard'), may hold values from -0.1875 to 0.1875
- w_rank: bfloat16 [16, 4, 128], P(None, 'head', 'shard'), may hold values from -1.5 to 1.5
- rank_bias: bfloat16 [4, 128], P('head', 'shard'), may hold values from -3 to 9
- head_gain: bfloat16 [256], P('shard'), may hold values from 0.25 to 1.75
- w_out: bfloat16 [1024, 1024], P('head', 'shard'), may hold values from -0.1875 to 0.1875
- mlp_gain: bfloat16 [1024], P('shard'), may hold values from 0.25 to 1.75
- w_gate: bfloat16 [1024, 2816], P('shard', 'head'), may hold values from -0.1875 to 0.1875
- w_up: bfloat16 [1024, 2816], P('shard', 'head'), may hold values from -0.1875 to 0.1875
- w_down: bfloat16 [2816, 1024], P('head', 'shard'), may hold values from -0.109375 to 0.109375
Outputs:
- resid_out: float32 [2048, 1024], P(('shard', 'head'))
- grad_in: float32 [2048, 1024], P(('shard', 'head'))
- grad_attn_gain: float32 [1024], P(('shard', 'head'))
- grad_w_query: float32 [1024, 512], P('shard', 'head')
- grad_w_key: float32 [1024, 512], P('shard', 'head')
- grad_w_value: float32 [1024, 1024], P('shard', 'head')
- grad_w_outgate: float32 [1024, 1024], P('shard', 'head')
- grad_w_low: float32 [1024, 16], P(('shard', 'head'))
- grad_w_rank: float32 [16, 4, 128], P(None, 'head', 'shard')
- grad_rank_bias: float32 [4, 128], P('head', 'shard')
- grad_head_gain: float32 [256], P(('shard', 'head'))
- grad_w_out: float32 [1024, 1024], P('head', 'shard')
- grad_mlp_gain: float32 [1024], P(('shard', 'head'))
- grad_w_gate: float32 [1024, 2816], P('shard', 'head')
- grad_w_up: float32 [1024, 2816], P('shard', 'head')
- grad_w_down: float32 [2816, 1024], P('head', 'shard')
The draws below stay inside these ranges and needn't reach their ends.
Inputs may be any that keep to these rules, and one draw needn't show every extreme that they name: `segment`: document ids never fall along the token stream; each id covers 1 to 1024 consecutive tokens and some id covers exactly 1024.
All inputs are finite; a program needn't handle non-finite values.
Results may differ from the reference program's by a relative error of at most 0.019.
Values may be sent and summed in bfloat16 or wider, within the bound.
A program may use at most 128 MiB of HBM per device.

```python
import math
import jax
import jax.numpy as jnp
import numpy as np
from jax import lax

D = 1024
HEADS = 4
DK = 128
DV = 256
GATE_RANK = 16
FF = 2816
GROUP = 64
SEQ = 1024
TOKENS = 2048


def raised(values, key, source, target, parts, factor):
    def block_of(position):
        return (jnp.arange(values.shape[position]) // (values.shape[position] // parts)).reshape((-1,) + (1,) * (values.ndim - 1 - position))

    first = jax.random.permutation(key, parts)[block_of(target)]
    far = (block_of(target) + parts // 2) % parts
    return jnp.where((block_of(source) == first) | (block_of(source) == far), factor * values, values)


def steps_of(key, shape, cuts, low, top_value):
    def one(axis_at, shards_of):
        draws = jax.random.uniform(jax.random.fold_in(jax.random.fold_in(key, 6), axis_at), (shards_of,), jnp.float32, low / len(cuts), top_value / len(cuts))
        return jnp.repeat(jnp.exp(draws), shape[axis_at] // shards_of).reshape((-1,) + (1,) * (len(shape) - axis_at - 1))

    factor_of = one(*cuts[0])
    for cut in cuts[1:]:
        factor_of = factor_of * one(*cut)
    return factor_of


def length_profile(number_of, total, most, slope):
    portions = [(1 << 20) // math.isqrt(standing ** slope) + 1 for standing in range(2, number_of + 1)]
    surplus, given = total - most - (number_of - 1), [1] * (number_of - 1)
    while surplus > 0:
        candidates = [i for i in range(number_of - 1) if given[i] < most]
        whole, left = sum([portions[i] for i in candidates]), surplus
        for i in candidates:
            addition = min(most - given[i], max(1, left * portions[i] // whole), surplus)
            given[i] = given[i] + addition
            surplus = surplus - addition
    return np.array([most] + given)


def ragged(rng, amount, total, most, slope):
    if amount == 2:
        one = jax.random.randint(rng, (), max(1, total - most), min(most, total - 1) + 1)
        return jnp.stack([one, total - one])
    tallies = jnp.asarray(length_profile(amount, total, most, slope), jnp.int32)
    couples = (amount - 1) // 2
    giver, sink = tallies[1:1 + 2 * couples:2], tallies[2:2 + 2 * couples:2]
    room = jnp.minimum(giver - 1, most - sink)
    moved = jax.random.randint(jax.random.fold_in(rng, 1), (couples,), 0, 1 << 20) % (room + 1)
    tallies = tallies.at[1:1 + 2 * couples:2].set(giver - moved).at[2:2 + 2 * couples:2].set(sink + moved)
    return tallies[jax.random.permutation(jax.random.fold_in(rng, 2), amount)]


def noise(own_key, extent, deviation, bound, cuts=(), held_as=jnp.bfloat16):
    values = deviation * jax.random.normal(own_key, extent, jnp.float32)
    if cuts:
        values = values * steps_of(own_key, extent, cuts, -0.22, 0.18)
    return jnp.clip(values, -bound, bound).astype(held_as)


def noise_with(own_key, dims, deviation, most, shards, heavy, held_as=jnp.bfloat16):
    entries = deviation * jax.random.normal(own_key, dims, jnp.float32)
    if shards:
        entries = entries * steps_of(own_key, dims, shards, -0.22, 0.18)
    return jnp.clip(raised(entries, jax.random.fold_in(own_key, 3), *heavy), -most, most).astype(held_as)


def setup_inputs(seed: int = 0) -> dict:
    streams_of = jax.random.split(jax.random.key(seed), 18)
    resid_in = noise(streams_of[0], (TOKENS, D), 1.0, 6.0, ((0, 32),), jnp.float32)
    cotangent = noise_with(streams_of[1], (TOKENS, D), 1.0, 6.0, ((0, 32),), (0, 1, 32, 2.75), jnp.float32)
    segment = jnp.searchsorted(jnp.cumsum(ragged(streams_of[2], 2 * TOKENS // SEQ, TOKENS, SEQ, 1)), jnp.arange(TOKENS), side="right").astype(jnp.int32)
    attn_gain = jnp.clip(1.0 + 0.15 * jax.random.normal(streams_of[3], (D,), jnp.float32), 0.25, 1.75).astype(jnp.bfloat16)
    w_query = noise(streams_of[4], (D, HEADS * DK), D ** -0.5, 0.1875, ((0, 8), (1, 4)))
    w_key = noise(streams_of[5], (D, HEADS * DK), D ** -0.5, 0.1875, ((0, 8), (1, 4)))
    w_value = noise(streams_of[6], (D, HEADS * DV), D ** -0.5, 0.1875, ((0, 8), (1, 4)))
    w_outgate = noise(streams_of[7], (D, HEADS * DV), D ** -0.5, 0.1875, ((0, 8), (1, 4)))
    w_low = noise(streams_of[8], (D, GATE_RANK), D ** -0.5, 0.1875, ((0, 8),))
    w_rank = noise(streams_of[9], (GATE_RANK, HEADS, DK), GATE_RANK ** -0.5, 1.5, ((1, 4), (2, 8)))
    rank_bias = jnp.clip(-3.0 + 12.0 * jax.random.uniform(streams_of[10], (HEADS, DK), jnp.float32) ** steps_of(streams_of[10], (HEADS, DK), ((0, 4), (1, 8)), -0.2, 0.2), -3.0, 9.0).astype(jnp.bfloat16)
    head_gain = jnp.clip(1.0 + 0.15 * jax.random.normal(streams_of[11], (DV,), jnp.float32), 0.25, 1.75).astype(jnp.bfloat16)
    w_out = noise(streams_of[12], (HEADS * DV, D), (HEADS * DV) ** -0.5, 0.1875, ((0, 4), (1, 8)))
    mlp_gain = jnp.clip(1.0 + 0.15 * jax.random.normal(streams_of[13], (D,), jnp.float32), 0.25, 1.75).astype(jnp.bfloat16)
    w_gate = noise(streams_of[14], (D, FF), D ** -0.5, 0.1875, ((0, 8), (1, 4)))
    w_up = noise(streams_of[15], (D, FF), D ** -0.5, 0.1875, ((0, 8), (1, 4)))
    w_down = noise(streams_of[16], (FF, D), FF ** -0.5, 0.109375, ((0, 4), (1, 8)))
    return dict(resid_in=resid_in, cotangent=cotangent, segment=segment, attn_gain=attn_gain, w_query=w_query, w_key=w_key, w_value=w_value, w_outgate=w_outgate, w_low=w_low, w_rank=w_rank, rank_bias=rank_bias, head_gain=head_gain, w_out=w_out, mlp_gain=mlp_gain, w_gate=w_gate, w_up=w_up, w_down=w_down)


EPS = 1e-06
HIGH_PRECISION = lax.Precision.HIGHEST

def rms_scale(values):
    return lax.rsqrt(lax.optimization_barrier(jnp.mean(values * values, axis=-1, keepdims=True)) + EPS)

def group_pass(query, key, value_rows, logdec, segf, state, carry_seg):
    total = query.shape[0]
    heads = query.shape[1]
    count = total // GROUP
    scale = DK ** (-0.5)
    order = jnp.arange(GROUP)
    causal = order[:, None] >= order[None, :]

    def blocks(array):
        return array.reshape((count, GROUP) + array.shape[1:])

    def advance(carry, pieces):
        memory_state, prior = carry
        query_c, key_c, value_segment, decay_c, seg_c = pieces
        cumul = jnp.cumsum(decay_c, axis=0)
        query_decayed = query_c * jnp.exp(cumul) * scale
        key_inc = key_c * jnp.exp(-cumul)
        scores = jnp.einsum('thk,shk->hts', query_decayed, key_inc, precision=HIGH_PRECISION)
        joined = jnp.logical_and(causal, seg_c[:, None] == seg_c[None, :])
        scores = jnp.where(joined[None], scores, 0.0)
        inherit = (seg_c == prior).astype(jnp.float32)
        inside = jnp.einsum('hts,shv->thv', scores, value_segment, precision=HIGH_PRECISION)
        carried_state = jnp.einsum('zsb,sbi->zsi', query_decayed, memory_state, precision=HIGH_PRECISION)
        result = inside + inherit[:, None, None] * carried_state
        final_result = cumul[-1]
        keep = (seg_c == seg_c[-1]).astype(jnp.float32)
        key_final_rows = key_c * jnp.exp(final_result[None] - cumul) * keep[:, None, None]
        linked_states = (seg_c[-1] == prior).astype(jnp.float32)
        memory_state = linked_states * jnp.exp(final_result)[:, :, None] * memory_state + jnp.einsum('zie,zir->ier', key_final_rows, value_segment, precision=HIGH_PRECISION)
        return ((memory_state, seg_c[-1]), result)
    (memory_state, last_seg), outs = lax.scan(advance, (state, carry_seg), (blocks(query), blocks(key), blocks(value_rows), blocks(logdec), blocks(segf)))
    return (outs.reshape(total, heads, outs.shape[-1]), memory_state)

def reference(resid_in, cotangent, segment, attn_gain, w_query, w_key, w_value, w_outgate, w_low, w_rank, rank_bias, head_gain, w_out, mlp_gain, w_gate, w_up, w_down):
    total = resid_in.shape[0]
    gain_attn = attn_gain.astype(jnp.float32)
    inv_attn = rms_scale(resid_in)
    normed_in = (resid_in * inv_attn * gain_attn).astype(jnp.bfloat16)
    query = jnp.dot(normed_in, w_query, preferred_element_type=jnp.float32).reshape(total, HEADS, DK)
    key = jnp.dot(normed_in, w_key, preferred_element_type=jnp.float32).reshape(total, HEADS, DK)
    value_rows = jnp.dot(normed_in, w_value, preferred_element_type=jnp.float32).reshape(total, HEADS, DV)
    outgate = jnp.dot(normed_in, w_outgate, preferred_element_type=jnp.float32).reshape(total, HEADS, DV)
    low = jnp.dot(normed_in, w_low, preferred_element_type=jnp.float32)
    rank_mat = w_rank.astype(jnp.float32).reshape(GATE_RANK, HEADS * DK)
    logit = jnp.dot(low, rank_mat, precision=HIGH_PRECISION) + rank_bias.astype(jnp.float32).reshape(HEADS * DK)
    logdec = (jax.nn.log_sigmoid(logit) / 16.0).reshape(total, HEADS, DK)
    segf = segment.astype(jnp.float32) + 1.0
    start_state = jnp.zeros((HEADS, DK, DV), jnp.float32)
    start_seg = jnp.zeros((), jnp.float32)

    def mixer(query_in, key_in, value_in, decay_in):
        return group_pass(query_in, key_in, value_in, decay_in, segf, start_state, start_seg)[0]
    mixed, mixer_back = jax.vjp(mixer, query, key, value_rows, logdec)
    inv_head = rms_scale(mixed)
    gain_head = head_gain.astype(jnp.float32)
    headnormed = mixed * inv_head * gain_head
    sigma_out = jax.nn.sigmoid(outgate)
    swish_out = outgate * sigma_out
    gated = (headnormed * swish_out).reshape(total, HEADS * DV).astype(jnp.bfloat16)
    resid_mid = resid_in + jnp.dot(gated, w_out, preferred_element_type=jnp.float32)
    width = math.gcd(total, 4096)
    nblocks = total // width
    gain_mlp = mlp_gain.astype(jnp.float32)

    def mlp_step(sums, rows):
        resid, cot = rows
        inv_mlp = rms_scale(resid)
        normed_mid = (resid * inv_mlp * gain_mlp).astype(jnp.bfloat16)
        gate_pre = jnp.dot(normed_mid, w_gate, preferred_element_type=jnp.float32)
        up_pre = jnp.dot(normed_mid, w_up, preferred_element_type=jnp.float32)
        sigma_gate = jax.nn.sigmoid(gate_pre)
        active = gate_pre * sigma_gate
        hidden = (active * up_pre).astype(jnp.bfloat16)
        result = resid + jnp.dot(hidden, w_down, preferred_element_type=jnp.float32)
        cot_bf = cot.astype(jnp.bfloat16)
        d_hidden = jnp.dot(cot_bf, w_down.T, preferred_element_type=jnp.float32)
        d_gatepre = (d_hidden * up_pre * sigma_gate * (1.0 + gate_pre * (1.0 - sigma_gate))).astype(jnp.bfloat16)
        d_uppre = (d_hidden * active).astype(jnp.bfloat16)
        grad_down = sums[0] + jnp.dot(hidden.T, cot_bf, preferred_element_type=jnp.float32)
        grad_gate = sums[1] + jnp.dot(normed_mid.T, d_gatepre, preferred_element_type=jnp.float32)
        grad_up = sums[2] + jnp.dot(normed_mid.T, d_uppre, preferred_element_type=jnp.float32)
        d_normmid = jnp.dot(d_gatepre, w_gate.T, preferred_element_type=jnp.float32) + jnp.dot(d_uppre, w_up.T, preferred_element_type=jnp.float32)
        grad_gain = sums[3] + lax.optimization_barrier(jnp.sum(d_normmid * resid * inv_mlp, axis=0))
        scaled = gain_mlp * d_normmid
        d_resid = cot + inv_mlp * scaled - resid * inv_mlp ** 3 * lax.optimization_barrier(jnp.mean(scaled * resid, axis=-1, keepdims=True))
        return ((grad_down, grad_gate, grad_up, grad_gain), (result, d_resid))
    start_sums = (jnp.zeros((FF, D), jnp.float32), jnp.zeros((D, FF), jnp.float32), jnp.zeros((D, FF), jnp.float32), jnp.zeros((D,), jnp.float32))
    sums, outs = lax.scan(mlp_step, start_sums, (resid_mid.reshape(nblocks, width, D), cotangent.reshape(nblocks, width, D)))
    grad_w_down, grad_w_gate, grad_w_up, grad_mlp_gain = sums
    resid_out = outs[0].reshape(total, D)
    d_mid = outs[1].reshape(total, D)
    dmid_bf = d_mid.astype(jnp.bfloat16)
    d_gated = jnp.dot(dmid_bf, w_out.T, preferred_element_type=jnp.float32).reshape(total, HEADS, DV)
    grad_w_out = jnp.dot(gated.T, dmid_bf, preferred_element_type=jnp.float32)
    d_head = d_gated * swish_out
    d_outgate = (d_gated * headnormed * sigma_out * (1.0 + outgate * (1.0 - sigma_out))).reshape(total, HEADS * DV).astype(jnp.bfloat16)
    grad_head_gain = lax.optimization_barrier(jnp.sum(d_head * mixed * inv_head, axis=(0, 1)))
    scaled_head = gain_head * d_head
    mixed_gradient = inv_head * scaled_head - mixed * inv_head ** 3 * lax.optimization_barrier(jnp.mean(scaled_head * mixed, axis=-1, keepdims=True))
    d_query, d_key, d_value, d_logdec = mixer_back(mixed_gradient)
    query_bf = d_query.reshape(total, HEADS * DK).astype(jnp.bfloat16)
    key_bf = d_key.reshape(total, HEADS * DK).astype(jnp.bfloat16)
    value_bf = d_value.reshape(total, HEADS * DV).astype(jnp.bfloat16)
    d_logit = d_logdec.reshape(total, HEADS * DK) * jax.nn.sigmoid(-logit) / 16.0
    grad_rank_bias = lax.optimization_barrier(jnp.sum(d_logit, axis=0)).reshape(HEADS, DK)
    grad_w_rank = jnp.dot(low.T, d_logit, precision=HIGH_PRECISION).reshape(GATE_RANK, HEADS, DK)
    d_low = jnp.einsum('thk,rhk->thr', d_logit.reshape(total, HEADS, DK), w_rank.astype(jnp.float32), precision=HIGH_PRECISION).astype(jnp.bfloat16).reshape(total, HEADS * GATE_RANK)
    grad_w_low = jnp.dot(normed_in.T, d_low, preferred_element_type=jnp.float32).reshape(D, HEADS, GATE_RANK).sum(axis=1)
    grad_w_query = jnp.dot(normed_in.T, query_bf, preferred_element_type=jnp.float32)
    grad_w_key = jnp.dot(normed_in.T, key_bf, preferred_element_type=jnp.float32)
    grad_w_value = jnp.dot(normed_in.T, value_bf, preferred_element_type=jnp.float32)
    grad_w_outgate = jnp.dot(normed_in.T, d_outgate, preferred_element_type=jnp.float32)
    low_rows = jnp.tile(w_low.T, (HEADS, 1))
    d_normin = jnp.dot(query_bf, w_query.T, preferred_element_type=jnp.float32)
    d_normin = d_normin + jnp.dot(key_bf, w_key.T, preferred_element_type=jnp.float32)
    d_normin = d_normin + jnp.dot(value_bf, w_value.T, preferred_element_type=jnp.float32)
    d_normin = d_normin + jnp.dot(d_outgate, w_outgate.T, preferred_element_type=jnp.float32)
    d_normin = d_normin + jnp.dot(d_low, low_rows, preferred_element_type=jnp.float32)
    grad_attn_gain = lax.optimization_barrier(jnp.sum(d_normin * resid_in * inv_attn, axis=0))
    scaled_in = gain_attn * d_normin
    grad_in = d_mid + inv_attn * scaled_in - resid_in * inv_attn ** 3 * lax.optimization_barrier(jnp.mean(scaled_in * resid_in, axis=-1, keepdims=True))
    return (resid_out, grad_in, grad_attn_gain, grad_w_query, grad_w_key, grad_w_value, grad_w_outgate, grad_w_low, grad_w_rank, grad_rank_bias, grad_head_gain, grad_w_out, grad_mlp_gain, grad_w_gate, grad_w_up, grad_w_down)
```

```python
import functools

import jax
import jax.numpy as jnp
from jax import lax
from jax.experimental import pallas as pl
from jax.experimental.pallas import tpu as pltpu
from jax.sharding import PartitionSpec as P

D = 1024
DK = 128
DV = 256
GATE_RANK = 16
GROUP = 64
LANE = 128
MESH = pl.DeviceIdType.MESH


EPS = 1e-06
HIGH_PRECISION = lax.Precision.HIGHEST


def ring_index(pos, n):
    return jnp.where(pos < n // 2, 2 * pos, 2 * (n - 1 - pos) + 1)


def ring_place(index, n):
    return jnp.where(index % 2 == 0, index // 2, n - 1 - index // 2)


def greet(axis, peers):
    barrier = pltpu.get_barrier_semaphore()
    for peer in peers:
        pl.semaphore_signal(barrier, inc=1, device_id={axis: peer}, device_id_type=MESH)
    pl.semaphore_wait(barrier, len(peers))


def cuts(columns, parts):
    lanes = columns // LANE
    sizes = [(lanes // parts + (1 if i < lanes % parts else 0)) * LANE for i in range(parts)]
    starts = [sum(sizes[:i]) for i in range(parts)]
    return list(zip(starts, sizes))


def ring_gather_kernel(n, axis, x_ref, o_ref, own_sem, send_sem, recv_sem):
    me = lax.axis_index(axis)
    pos = ring_place(me, n)
    right = ring_index((pos + 1) % n, n)
    left = ring_index((pos + n - 1) % n, n)
    greet(axis, (left, right))
    own = pltpu.make_async_copy(x_ref, o_ref.at[me], own_sem)
    own.start()
    pieces = cuts(x_ref.shape[1], 2)
    steps = n // 2
    sent = {}
    for step in range(steps):
        for part, (start, size) in enumerate(pieces):
            for way in range(2):
                if step == steps - 1 and part != way:
                    continue
                shift = n - step if way == 0 else step
                block = ring_index((pos + shift) % n, n)
                columns = pl.ds(start, size)
                if step > 0:
                    sent[(step - 1, part, way)].wait_recv()
                source = x_ref.at[:, columns] if step == 0 else o_ref.at[block, :, columns]
                copy = pltpu.make_async_remote_copy(
                    src_ref=source,
                    dst_ref=o_ref.at[block, :, columns],
                    send_sem=send_sem.at[step, part, way],
                    recv_sem=recv_sem.at[step, part, way],
                    device_id={axis: right if way == 0 else left},
                    device_id_type=MESH,
                )
                copy.start()
                sent[(step, part, way)] = copy
    for (step, part, way), copy in sent.items():
        if (step + 1, part, way) not in sent:
            copy.wait_recv()
    for copy in sent.values():
        copy.wait_send()
    own.wait()


def ring_gather(x, axis, ident):
    n = lax.axis_size(axis)
    return pl.pallas_call(
        functools.partial(ring_gather_kernel, n, axis),
        out_shape=jax.ShapeDtypeStruct((n,) + x.shape, x.dtype),
        in_specs=[pl.BlockSpec(memory_space=pltpu.VMEM)],
        out_specs=pl.BlockSpec(memory_space=pl.ANY),
        scratch_shapes=[
            pltpu.SemaphoreType.DMA,
            pltpu.SemaphoreType.DMA((n // 2, 2, 2)),
            pltpu.SemaphoreType.DMA((n // 2, 2, 2)),
        ],
        compiler_params=pltpu.CompilerParams(collective_id=ident, has_side_effects=True),
    )(x)


def ring_sum_kernel(n, axis, g_ref, o_ref, held, send_sem, recv_sem):
    me = lax.axis_index(axis)
    pos = ring_place(me, n)
    right = ring_index((pos + 1) % n, n)
    left = ring_index((pos + n - 1) % n, n)
    greet(axis, (left, right))
    pieces = cuts(g_ref.shape[2], 4)

    def copy_of(step, part, source):
        way = part % 2
        start, size = pieces[part]
        return pltpu.make_async_remote_copy(
            src_ref=source,
            dst_ref=held.at[step, :, pl.ds(start, size)],
            send_sem=send_sem.at[step, part],
            recv_sem=recv_sem.at[step, part],
            device_id={axis: right if way == 0 else left},
            device_id_type=MESH,
        )

    def block_of(step, part):
        shift = 2 * n - 1 - step if part % 2 == 0 else 1 + step
        return ring_index((pos + shift) % n, n)

    for part, (start, size) in enumerate(pieces):
        copy_of(0, part, g_ref.at[block_of(0, part), :, pl.ds(start, size)]).start()

    def one(step, carry):
        for part, (start, size) in enumerate(pieces):
            columns = pl.ds(start, size)
            slot = held.at[step - 1, :, columns]
            copy_of(step - 1, part, slot).wait_recv()
            held[step - 1, :, columns] = (
                held[step - 1, :, columns].astype(jnp.float32)
                + g_ref[block_of(step, part), :, columns].astype(jnp.float32)
            ).astype(held.dtype)
            copy_of(step, part, slot).start()
        return carry

    lax.fori_loop(1, n - 1, one, 0)
    for part, (start, size) in enumerate(pieces):
        columns = pl.ds(start, size)
        copy_of(n - 2, part, held.at[n - 2, :, columns]).wait_recv()
        o_ref[:, columns] = held[n - 2, :, columns].astype(jnp.float32) + g_ref[
            me, :, columns
        ].astype(jnp.float32)

    def drain(step, carry):
        for part, (start, size) in enumerate(pieces):
            copy_of(step, part, held.at[step, :, pl.ds(start, size)]).wait_send()
        return carry

    lax.fori_loop(0, n - 1, drain, 0)


def ring_sum(g, axis, ident):
    n, rows, columns = g.shape
    return pl.pallas_call(
        functools.partial(ring_sum_kernel, n, axis),
        out_shape=jax.ShapeDtypeStruct((rows, columns), jnp.float32),
        in_specs=[pl.BlockSpec(memory_space=pltpu.VMEM)],
        out_specs=pl.BlockSpec(memory_space=pltpu.VMEM),
        scratch_shapes=[
            pltpu.VMEM((n - 1, rows, columns), g.dtype),
            pltpu.SemaphoreType.DMA((n - 1, 4)),
            pltpu.SemaphoreType.DMA((n - 1, 4)),
        ],
        compiler_params=pltpu.CompilerParams(collective_id=ident, has_side_effects=True),
    )(g)


def gather_kernel(n, axis, x_ref, o_ref, send_sem, recv_sem):
    me = lax.axis_index(axis)
    peers = [(me + k) % n for k in range(1, n)]
    greet(axis, peers)
    copies = []
    for k, peer in enumerate(peers):
        copy = pltpu.make_async_remote_copy(
            src_ref=x_ref,
            dst_ref=o_ref.at[me],
            send_sem=send_sem.at[k],
            recv_sem=recv_sem.at[k],
            device_id={axis: peer},
            device_id_type=MESH,
        )
        copy.start()
        copies.append(copy)
    o_ref[me] = x_ref[...]
    for copy in copies:
        copy.wait()


def gather(x, axis, ident):
    n = lax.axis_size(axis)
    return pl.pallas_call(
        functools.partial(gather_kernel, n, axis),
        out_shape=jax.ShapeDtypeStruct((n,) + x.shape, x.dtype),
        in_specs=[pl.BlockSpec(memory_space=pltpu.VMEM)],
        out_specs=pl.BlockSpec(memory_space=pltpu.VMEM),
        scratch_shapes=[
            pltpu.SemaphoreType.DMA((n - 1,)),
            pltpu.SemaphoreType.DMA((n - 1,)),
        ],
        compiler_params=pltpu.CompilerParams(collective_id=ident, has_side_effects=True),
    )(x)


def scatter_sum_kernel(n, axis, x_ref, o_ref, held, send_sem, recv_sem):
    me = lax.axis_index(axis)
    peers = [(me + k) % n for k in range(1, n)]
    greet(axis, peers)
    copies = []
    for k, peer in enumerate(peers):
        copy = pltpu.make_async_remote_copy(
            src_ref=x_ref.at[peer],
            dst_ref=held.at[k],
            send_sem=send_sem.at[k],
            recv_sem=recv_sem.at[k],
            device_id={axis: peer},
            device_id_type=MESH,
        )
        copy.start()
        copies.append(copy)
    for copy in copies:
        copy.wait()
    total = x_ref[me].astype(jnp.float32)
    for k in range(n - 1):
        total = total + held[k].astype(jnp.float32)
    o_ref[...] = total


def scatter_sum(x, axis, ident):
    n = lax.axis_size(axis)
    rows, columns = x.shape[0] // n, x.shape[1]
    return pl.pallas_call(
        functools.partial(scatter_sum_kernel, n, axis),
        out_shape=jax.ShapeDtypeStruct((rows, columns), jnp.float32),
        in_specs=[pl.BlockSpec(memory_space=pltpu.VMEM)],
        out_specs=pl.BlockSpec(memory_space=pltpu.VMEM),
        scratch_shapes=[
            pltpu.VMEM((n - 1, rows, columns), x.dtype),
            pltpu.SemaphoreType.DMA((n - 1,)),
            pltpu.SemaphoreType.DMA((n - 1,)),
        ],
        compiler_params=pltpu.CompilerParams(collective_id=ident, has_side_effects=True),
    )(x.reshape(n, rows, columns))


def chain(decay, state, first, last, backward, ident):
    n = lax.axis_size("shard")
    me = lax.axis_index("shard")
    lines = jnp.zeros((16, DV), jnp.float32)
    lines = lines.at[0, :DK].set(decay).at[1, 0].set(first).at[1, 1].set(last)
    block = jnp.concatenate([state, lines], axis=0).astype(jnp.bfloat16)
    every = gather(block, "shard", ident)
    states = every[:, :DK].astype(jnp.float32)
    decays = every[:, DK, :DK].astype(jnp.float32)
    firsts = every[:, DK + 1, 0].astype(jnp.float32)
    lasts = every[:, DK + 1, 1].astype(jnp.float32)
    place = jnp.arange(n)
    j, i = place[:, None], place[None, :]
    if backward:
        passing = decays
        between = jnp.logical_and(i > me, i < j)
        counted = place > me
    else:
        before = jnp.concatenate([jnp.zeros((1,), jnp.float32), lasts[:-1]])
        passing = decays * (firsts == before).astype(jnp.float32)[:, None]
        between = jnp.logical_and(i > j, i < me)
        counted = place < me
    weight = jnp.prod(jnp.where(between[:, :, None], passing[None], 1.0), axis=1)
    weight = jnp.where(counted[:, None], weight, 0.0)
    incoming = jnp.sum(weight[:, :, None] * states, axis=0)
    prior = jnp.sum(jnp.where(place == me - 1, lasts, 0.0))
    return incoming[None], prior


def rms_scale(values):
    return lax.rsqrt(jnp.mean(values * values, axis=-1, keepdims=True) + EPS)


def group_pass(query, key, value_rows, logdec, segf, state, carry_seg):
    total = query.shape[0]
    heads = query.shape[1]
    count = total // GROUP
    scale = DK ** (-0.5)
    order = jnp.arange(GROUP)
    causal = order[:, None] >= order[None, :]

    def blocks(array):
        return array.reshape((count, GROUP) + array.shape[1:])

    def advance(carry, pieces):
        memory_state, prior = carry
        query_c, key_c, value_segment, decay_c, seg_c = pieces
        cumul = jnp.cumsum(decay_c, axis=0)
        query_decayed = query_c * jnp.exp(cumul) * scale
        key_inc = key_c * jnp.exp(-cumul)
        scores = jnp.einsum("thk,shk->hts", query_decayed, key_inc, precision=HIGH_PRECISION)
        joined = jnp.logical_and(causal, seg_c[:, None] == seg_c[None, :])
        scores = jnp.where(joined[None], scores, 0.0)
        inherit = (seg_c == prior).astype(jnp.float32)
        inside = jnp.einsum("hts,shv->thv", scores, value_segment, precision=HIGH_PRECISION)
        carried_state = jnp.einsum(
            "zsb,sbi->zsi", query_decayed, memory_state, precision=HIGH_PRECISION
        )
        result = inside + inherit[:, None, None] * carried_state
        final_result = cumul[-1]
        keep = (seg_c == seg_c[-1]).astype(jnp.float32)
        key_final_rows = key_c * jnp.exp(final_result[None] - cumul) * keep[:, None, None]
        linked_states = (seg_c[-1] == prior).astype(jnp.float32)
        memory_state = linked_states * jnp.exp(final_result)[
            :, :, None
        ] * memory_state + jnp.einsum(
            "zie,zir->ier", key_final_rows, value_segment, precision=HIGH_PRECISION
        )
        return ((memory_state, seg_c[-1]), result)

    (memory_state, last_seg), outs = lax.scan(
        advance,
        (state, carry_seg),
        (blocks(query), blocks(key), blocks(value_rows), blocks(logdec), blocks(segf)),
        unroll=True,
    )
    return (outs.reshape(total, heads, outs.shape[-1]), memory_state)


def on_device(
    resid_in,
    cotangent,
    segment,
    attn_gain,
    w_query,
    w_key,
    w_value,
    w_outgate,
    w_low,
    w_rank,
    rank_bias,
    head_gain,
    w_out,
    mlp_gain,
    w_gate,
    w_up,
    w_down,
):

    n = lax.axis_size("shard")
    wide = w_gate.shape[1]
    rows = w_query.shape[0]

    def tall(a):
        a = a.reshape(a.shape[0], -1)
        return jnp.pad(a, ((0, rows - a.shape[0]), (0, 0)))

    packed = jnp.concatenate(
        [
            w_query,
            w_key,
            w_value,
            w_outgate,
            w_out.T,
            w_gate,
            w_up,
            w_down.T,
            w_low,
            tall(attn_gain),
            tall(mlp_gain),
            tall(head_gain),
            tall(w_rank[:, 0, :].T),
            tall(rank_bias[0]),
        ],
        axis=1,
    )
    used = packed.shape[1]
    packed = jnp.pad(packed, ((0, 0), (0, -used % LANE)))
    every = ring_gather(packed, "shard", 1)
    spread = every.reshape(n * rows, packed.shape[1])
    edge_out = 2 * DK + 2 * DV
    edge_gate = edge_out + DV
    edge_down = edge_gate + 2 * wide
    edge_low = edge_down + wide
    project_w = spread[:, :edge_out]
    out_wt = spread[:, edge_out:edge_gate]
    gu_w = spread[:, edge_gate:edge_down]
    down_wt = spread[:, edge_down:edge_low]
    tail = every[:, :, edge_low:]
    low_w = tail[:, :, :GATE_RANK].reshape(D, GATE_RANK)
    gain_attn = tail[:, :, GATE_RANK].reshape(D).astype(jnp.float32)
    gain_mlp = tail[:, :, GATE_RANK + 1].reshape(D).astype(jnp.float32)
    gain_head = tail[:, : DV // n, GATE_RANK + 2].reshape(DV).astype(jnp.float32)
    rank_w = tail[:, : DK // n, GATE_RANK + 3 : 2 * GATE_RANK + 3].reshape(DK, GATE_RANK).T
    bias_w = tail[:, : DK // n, 2 * GATE_RANK + 3].reshape(DK)
    length = segment.shape[0]
    local_heads = 1
    scale = DK ** (-0.5)
    inv_attn = rms_scale(resid_in)
    normed_rows = (resid_in * inv_attn * gain_attn).astype(jnp.bfloat16)
    cot_rows = cotangent.astype(jnp.bfloat16)
    both = gather(jnp.concatenate([normed_rows, cot_rows], axis=1), "head", 2)
    normed_in = both[:, :, :D].reshape(length, D)
    cot_bf = both[:, :, D:].reshape(length, D)
    projected = jnp.dot(normed_in, project_w, preferred_element_type=jnp.float32)
    query = projected[:, :DK].reshape(length, local_heads, DK)
    key = projected[:, DK : 2 * DK].reshape(length, local_heads, DK)
    value_rows = projected[:, 2 * DK : 2 * DK + DV].reshape(length, local_heads, DV)
    outgate = projected[:, 2 * DK + DV :].reshape(length, local_heads, DV)
    low = jnp.dot(normed_in, low_w, preferred_element_type=jnp.float32)
    rank_mat = rank_w.astype(jnp.float32).reshape(GATE_RANK, local_heads * DK)
    logit = jnp.dot(low, rank_mat, precision=HIGH_PRECISION) + bias_w.astype(jnp.float32).reshape(
        local_heads * DK
    )
    logdec = (jax.nn.log_sigmoid(logit) / 16.0).reshape(length, local_heads, DK)
    segf = segment.astype(jnp.float32) + 1.0
    first_seg = segf[:1]
    last_seg = segf[-1:]
    cumul = jnp.cumsum(logdec, axis=0)
    keep = (segf == last_seg[0]).astype(jnp.float32)
    key_final_rows = key * jnp.exp(cumul[-1][None] - cumul) * keep[:, None, None]
    summary_state = jnp.einsum("zie,zir->ier", key_final_rows, value_rows, precision=HIGH_PRECISION)
    through = jnp.exp(cumul[-1]) * (first_seg[0] == last_seg[0]).astype(jnp.float32)
    state_in, prior = chain(through[0], summary_state[0], first_seg[0], last_seg[0], False, 3)

    def mixer(query_in, key_in, value_in, decay_in):
        return group_pass(query_in, key_in, value_in, decay_in, segf, state_in, prior)

    (mixed, state_out), mixer_back = jax.vjp(mixer, query, key, value_rows, logdec)
    inv_head = rms_scale(mixed)
    headnormed = mixed * inv_head * gain_head
    sigma_out = jax.nn.sigmoid(outgate)
    swish_out = outgate * sigma_out
    gated = (headnormed * swish_out).reshape(length, local_heads * DV).astype(jnp.bfloat16)
    resid_mid = resid_in + scatter_sum(
        jnp.dot(gated, out_wt.T, preferred_element_type=jnp.float32).astype(jnp.bfloat16),
        "head",
        4,
    )
    inv_mlp = rms_scale(resid_mid)
    mid_rows = (resid_mid * inv_mlp * gain_mlp).astype(jnp.bfloat16)
    normed_mid = gather(mid_rows, "head", 5).reshape(length, D)
    gate_up = jnp.dot(normed_mid, gu_w, preferred_element_type=jnp.float32)
    gate_pre = gate_up[:, :wide]
    up_pre = gate_up[:, wide:]
    sigma_gate = jax.nn.sigmoid(gate_pre)
    active = gate_pre * sigma_gate
    hidden = (active * up_pre).astype(jnp.bfloat16)
    d_hidden = jnp.dot(cot_bf, down_wt, preferred_element_type=jnp.float32)
    d_gatepre = (d_hidden * up_pre * sigma_gate * (1.0 + gate_pre * (1.0 - sigma_gate))).astype(
        jnp.bfloat16
    )
    d_uppre = (d_hidden * active).astype(jnp.bfloat16)
    d_gu = jnp.concatenate([d_gatepre, d_uppre], axis=1)
    grad_down = jnp.dot(cot_bf.T, hidden, preferred_element_type=jnp.float32)
    grad_gu = jnp.dot(normed_mid.T, d_gu, preferred_element_type=jnp.float32)
    shares = jnp.concatenate(
        [
            jnp.dot(hidden, down_wt.T, preferred_element_type=jnp.float32).astype(jnp.bfloat16),
            jnp.dot(d_gu, gu_w.T, preferred_element_type=jnp.float32).astype(jnp.bfloat16),
        ],
        axis=1,
    )
    summed = scatter_sum(shares, "head", 6)
    resid_out = resid_mid + summed[:, :D]
    d_normmid = summed[:, D:]
    part_mlp_gain = jnp.sum(d_normmid * resid_mid * inv_mlp, axis=0)
    scaled_mid = gain_mlp * d_normmid
    d_mid = (
        cotangent
        + inv_mlp * scaled_mid
        - resid_mid * inv_mlp**3 * jnp.mean(scaled_mid * resid_mid, axis=-1, keepdims=True)
    )
    dmid_rows = d_mid.astype(jnp.bfloat16)
    dmid_bf = gather(dmid_rows, "head", 7).reshape(length, D)
    d_gated = jnp.dot(dmid_bf, out_wt, preferred_element_type=jnp.float32).reshape(
        length, local_heads, DV
    )
    grad_out = jnp.dot(dmid_bf.T, gated, preferred_element_type=jnp.float32)
    d_head = d_gated * swish_out
    d_outgate = (
        (d_gated * headnormed * sigma_out * (1.0 + outgate * (1.0 - sigma_out)))
        .reshape(length, local_heads * DV)
        .astype(jnp.bfloat16)
    )
    part_head_gain = jnp.sum(d_head * mixed * inv_head, axis=(0, 1))
    scaled_head = gain_head * d_head
    mixed_gradient = inv_head * scaled_head - mixed * inv_head**3 * jnp.mean(
        scaled_head * mixed, axis=-1, keepdims=True
    )
    inherit = (segf == prior).astype(jnp.float32)
    weighted_query = query * jnp.exp(cumul) * inherit[:, None, None] * scale
    local_gradient = jnp.einsum(
        "zie,zir->ier", weighted_query, mixed_gradient, precision=HIGH_PRECISION
    )
    through_all = jnp.exp(cumul[-1]) * (last_seg[0] == prior).astype(jnp.float32)
    nothing = jnp.zeros((), jnp.float32)
    outgoing, _ = chain(through_all[0], local_gradient[0], nothing, nothing, True, 8)
    d_query, d_key, d_value, d_logdec = mixer_back((mixed_gradient, outgoing))
    query_bf = d_query.reshape(length, local_heads * DK).astype(jnp.bfloat16)
    key_bf = d_key.reshape(length, local_heads * DK).astype(jnp.bfloat16)
    value_bf = d_value.reshape(length, local_heads * DV).astype(jnp.bfloat16)
    d_logit = d_logdec.reshape(length, local_heads * DK) * jax.nn.sigmoid(-logit) / 16.0
    grad_bias = jnp.sum(d_logit, axis=0).reshape(local_heads, DK)
    grad_rank = jnp.dot(low.T, d_logit, precision=HIGH_PRECISION).reshape(
        GATE_RANK, local_heads, DK
    )
    d_low = (
        jnp.einsum(
            "thk,rhk->thr",
            d_logit.reshape(length, local_heads, DK),
            rank_w.astype(jnp.float32).reshape(GATE_RANK, local_heads, DK),
            precision=HIGH_PRECISION,
        )
        .astype(jnp.bfloat16)
        .reshape(length, local_heads * GATE_RANK)
    )
    part_low = (
        jnp.dot(normed_in.T, d_low, preferred_element_type=jnp.float32)
        .reshape(D, local_heads, GATE_RANK)
        .sum(axis=1)
    )
    d_project = jnp.concatenate([query_bf, key_bf, value_bf, d_outgate], axis=1)
    grad_project = jnp.dot(normed_in.T, d_project, preferred_element_type=jnp.float32)
    low_rows = low_w.T
    total_term = jnp.dot(d_project, project_w.T, preferred_element_type=jnp.float32)
    d_normin = scatter_sum(
        (total_term + jnp.dot(d_low, low_rows, preferred_element_type=jnp.float32)).astype(
            jnp.bfloat16
        ),
        "head",
        9,
    )
    part_attn_gain = jnp.sum(d_normin * resid_in * inv_attn, axis=0)
    scaled_in = gain_attn * d_normin
    grad_in = (
        d_mid
        + inv_attn * scaled_in
        - resid_in * inv_attn**3 * jnp.mean(scaled_in * resid_in, axis=-1, keepdims=True)
    )

    def owners(a):
        a = a.reshape(n, a.shape[0] // n, -1)
        return jnp.pad(a, ((0, 0), (0, rows - a.shape[1]), (0, 0))).reshape(D, -1)

    grads = jnp.concatenate(
        [
            g.astype(jnp.bfloat16)
            for g in (
                grad_project,
                grad_out,
                grad_gu,
                grad_down,
                part_low,
                part_attn_gain[:, None],
                part_mlp_gain[:, None],
                owners(part_head_gain),
                owners(grad_rank[:, 0, :].T),
                owners(grad_bias[0]),
            )
        ],
        axis=1,
    )
    grads = jnp.pad(grads, ((0, 0), (0, packed.shape[1] - used)))
    owned = ring_sum(grads.reshape(n, rows, packed.shape[1]), "shard", 10)
    heads = lax.axis_size("head")
    shared = owned[:, edge_low : edge_low + GATE_RANK + 3]
    gain_rows = DV // n
    final_rank = owned[: DK // n, edge_low + GATE_RANK + 3 : edge_low + 2 * GATE_RANK + 3]
    final_bias = owned[: DK // n, edge_low + 2 * GATE_RANK + 3]
    shares = jnp.concatenate(
        [
            shared[:, : GATE_RANK + 2].reshape(heads, rows // heads, GATE_RANK + 2),
            jnp.pad(
                shared[:gain_rows, GATE_RANK + 2].reshape(heads, gain_rows // heads, 1),
                ((0, 0), (0, (rows - gain_rows) // heads), (0, 0)),
            ),
        ],
        axis=2,
    )
    deep = max(rows // heads, 16)
    shares = jnp.pad(
        shares, ((0, 0), (0, deep - rows // heads), (0, LANE - GATE_RANK - 3))
    ).reshape(heads * deep, LANE)
    final = scatter_sum(shares.astype(jnp.bfloat16), "head", 11)[: rows // heads]
    return (
        resid_out,
        grad_in,
        final[:, GATE_RANK],
        owned[:, :DK],
        owned[:, DK : 2 * DK],
        owned[:, 2 * DK : 2 * DK + DV],
        owned[:, 2 * DK + DV : edge_out],
        final[:, :GATE_RANK],
        final_rank.T.reshape(GATE_RANK, 1, DK // n),
        final_bias.reshape(1, DK // n),
        final[: gain_rows // heads, GATE_RANK + 2],
        owned[:, edge_out:edge_gate].T,
        final[:, GATE_RANK + 1],
        owned[:, edge_gate : edge_gate + wide],
        owned[:, edge_gate + wide : edge_down],
        owned[:, edge_down:edge_low].T,
    )


def solution(mesh):
    in_specs = (
        P(("shard", "head"), None),
        P(("shard", "head"), None),
        P("shard"),
        P("shard"),
        P("shard", "head"),
        P("shard", "head"),
        P("shard", "head"),
        P("shard", "head"),
        P("shard", None),
        P(None, "head", "shard"),
        P("head", "shard"),
        P("shard"),
        P("head", "shard"),
        P("shard"),
        P("shard", "head"),
        P("shard", "head"),
        P("head", "shard"),
    )
    out_specs = (
        P(("shard", "head"), None),
        P(("shard", "head"), None),
        P(("shard", "head")),
        P("shard", "head"),
        P("shard", "head"),
        P("shard", "head"),
        P("shard", "head"),
        P(("shard", "head"), None),
        P(None, "head", "shard"),
        P("head", "shard"),
        P(("shard", "head")),
        P("head", "shard"),
        P(("shard", "head")),
        P("shard", "head"),
        P("shard", "head"),
        P("head", "shard"),
    )
    return jax.shard_map(
        on_device, mesh=mesh, in_specs=in_specs, out_specs=out_specs, check_vma=False
    )
```

```python
import functools

import jax
import jax.numpy as jnp
from jax import lax
from jax.experimental import pallas as pl
from jax.experimental.pallas import tpu as pltpu
from jax.sharding import PartitionSpec as P

D = 1024
DK = 128
DV = 256
GATE_RANK = 16
GROUP = 64
LANE = 128
MESH = pl.DeviceIdType.MESH


EPS = 1e-06
HIGH_PRECISION = lax.Precision.HIGHEST


def ring_index(pos, n):
    return jnp.where(pos < n // 2, 2 * pos, 2 * (n - 1 - pos) + 1)


def ring_place(index, n):
    return jnp.where(index % 2 == 0, index // 2, n - 1 - index // 2)


def greet(*pairs):
    barrier = pltpu.get_barrier_semaphore()
    for axis, peer in pairs:
        pl.semaphore_signal(barrier, inc=1, device_id={axis: peer}, device_id_type=MESH)
    pl.semaphore_wait(barrier, len(pairs))


def remote(source, target, send_sem, recv_sem, axis, peer):
    return pltpu.make_async_remote_copy(
        src_ref=source,
        dst_ref=target,
        send_sem=send_sem,
        recv_sem=recv_sem,
        device_id={axis: peer},
        device_id_type=MESH,
    )


def quad(axis):
    me = lax.axis_index(axis)
    return me, me + 1 - 2 * (me % 2), (me + 2) % 4


def cuts(columns, parts):
    lanes = columns // LANE
    sizes = [(lanes // parts + (1 if i < lanes % parts else 0)) * LANE for i in range(parts)]
    starts = [sum(sizes[:i]) for i in range(parts)]
    return list(zip(starts, sizes))


def ring_gather_kernel(n, axis, x_ref, o_ref, own_sem, send_sem, recv_sem):
    right, left = ring_sides(n, axis)
    greet((axis, left), (axis, right))
    ring_gather_body(n, axis, x_ref, o_ref, own_sem, send_sem, recv_sem, None)


def ring_sides(n, axis):
    pos = ring_place(lax.axis_index(axis), n)
    return ring_index((pos + 1) % n, n), ring_index((pos + n - 1) % n, n)


def ring_gather_body(n, axis, x_ref, o_ref, own_sem, send_sem, recv_sem, meanwhile):
    me = lax.axis_index(axis)
    pos = ring_place(me, n)
    right, left = ring_sides(n, axis)
    own = pltpu.make_async_copy(x_ref, o_ref.at[me], own_sem)
    own.start()
    pieces = cuts(x_ref.shape[1], 2)
    steps = n // 2
    sent = {}
    for step in range(steps):
        for part, (start, size) in enumerate(pieces):
            for way in range(2):
                if step == steps - 1 and part != way:
                    continue
                shift = n - step if way == 0 else step
                block = ring_index((pos + shift) % n, n)
                columns = pl.ds(start, size)
                if step > 0:
                    sent[(step - 1, part, way)].wait_recv()
                source = x_ref.at[:, columns] if step == 0 else o_ref.at[block, :, columns]
                copy = pltpu.make_async_remote_copy(
                    src_ref=source,
                    dst_ref=o_ref.at[block, :, columns],
                    send_sem=send_sem.at[step, part, way],
                    recv_sem=recv_sem.at[step, part, way],
                    device_id={axis: right if way == 0 else left},
                    device_id_type=MESH,
                )
                copy.start()
                sent[(step, part, way)] = copy
        if step == 0 and meanwhile is not None:
            meanwhile()
    for (step, part, way), copy in sent.items():
        if (step + 1, part, way) not in sent:
            copy.wait_recv()
    for copy in sent.values():
        copy.wait_send()
    own.wait()


def ring_gather(x, axis, ident):
    n = lax.axis_size(axis)
    return pl.pallas_call(
        functools.partial(ring_gather_kernel, n, axis),
        out_shape=jax.ShapeDtypeStruct((n,) + x.shape, x.dtype),
        in_specs=[pl.BlockSpec(memory_space=pltpu.VMEM)],
        out_specs=pl.BlockSpec(memory_space=pl.ANY),
        scratch_shapes=[
            pltpu.SemaphoreType.DMA,
            pltpu.SemaphoreType.DMA((n // 2, 2, 2)),
            pltpu.SemaphoreType.DMA((n // 2, 2, 2)),
        ],
        compiler_params=pltpu.CompilerParams(collective_id=ident, has_side_effects=True),
    )(x)


def quad_gather_parts(axis, x_ref, o_ref, send_sem, recv_sem):
    me, beside, across = quad(axis)
    half = x_ref.shape[0] // 2
    parts = [pl.ds(0, half), pl.ds(half, half)]
    first = [
        (
            remote(x_ref.at[rows], o_ref.at[me, rows], send_sem.at[i, 0], recv_sem.at[i, 0], axis, across),
            remote(x_ref.at[rows], o_ref.at[me, rows], send_sem.at[i, 1], recv_sem.at[i, 1], axis, beside),
        )
        for i, rows in enumerate(parts)
    ]
    onward = [
        remote(
            o_ref.at[across, rows],
            o_ref.at[across, rows],
            send_sem.at[i, 2],
            recv_sem.at[i, 2],
            axis,
            beside,
        )
        for i, rows in enumerate(parts)
    ]

    def start():
        for far, near in first:
            far.start()
            near.start()
        o_ref[me] = x_ref[...]

    def relay():
        for (far, _), more in zip(first, onward):
            far.wait_recv()
            more.start()

    def finish():
        for (far, near), more in zip(first, onward):
            near.wait_recv()
            more.wait_recv()
            far.wait_send()
            near.wait_send()
            more.wait_send()

    return start, relay, finish


def gather_kernel(axis, x_ref, o_ref, send_sem, recv_sem):
    _, beside, across = quad(axis)
    greet((axis, beside), (axis, across))
    start, relay, finish = quad_gather_parts(axis, x_ref, o_ref, send_sem, recv_sem)
    start()
    relay()
    finish()


def gather(x, axis, ident):
    return pl.pallas_call(
        functools.partial(gather_kernel, axis),
        out_shape=jax.ShapeDtypeStruct((4,) + x.shape, x.dtype),
        in_specs=[pl.BlockSpec(memory_space=pltpu.VMEM)],
        out_specs=pl.BlockSpec(memory_space=pltpu.VMEM),
        scratch_shapes=[
            pltpu.SemaphoreType.DMA((2, 3)),
            pltpu.SemaphoreType.DMA((2, 3)),
        ],
        compiler_params=pltpu.CompilerParams(collective_id=ident, has_side_effects=True),
    )(x)


def enter_kernel(n, w_ref, x_ref, spread_ref, o_ref, own_sem, send_w, recv_w, send_x, recv_x):
    right, left = ring_sides(n, "shard")
    _, beside, across = quad("head")
    greet(("shard", left), ("shard", right), ("head", beside), ("head", across))
    start, relay, finish = quad_gather_parts("head", x_ref, o_ref, send_x, recv_x)
    start()
    ring_gather_body(n, "shard", w_ref, spread_ref, own_sem, send_w, recv_w, relay)
    finish()


def enter(weights, x, ident):
    n = lax.axis_size("shard")
    return pl.pallas_call(
        functools.partial(enter_kernel, n),
        out_shape=(
            jax.ShapeDtypeStruct((n,) + weights.shape, weights.dtype),
            jax.ShapeDtypeStruct((4,) + x.shape, x.dtype),
        ),
        in_specs=[pl.BlockSpec(memory_space=pltpu.VMEM)] * 2,
        out_specs=(
            pl.BlockSpec(memory_space=pl.ANY),
            pl.BlockSpec(memory_space=pltpu.VMEM),
        ),
        scratch_shapes=[
            pltpu.SemaphoreType.DMA,
            pltpu.SemaphoreType.DMA((n // 2, 2, 2)),
            pltpu.SemaphoreType.DMA((n // 2, 2, 2)),
            pltpu.SemaphoreType.DMA((2, 3)),
            pltpu.SemaphoreType.DMA((2, 3)),
        ],
        compiler_params=pltpu.CompilerParams(collective_id=ident, has_side_effects=True),
    )(weights, x)


def ring_sum_kernel(n, axis, pieces, count, *refs):
    g_refs, o_refs = refs[:count], refs[count : 2 * count]
    held, send_sem, recv_sem = refs[2 * count :]
    me = lax.axis_index(axis)
    pos = ring_place(me, n)
    right, left = ring_sides(n, axis)
    greet((axis, left), (axis, right))

    def slot_of(step, part):
        start, size = pieces[part][3:]
        return held.at[step, :, pl.ds(start, size)]

    def copy_of(step, part, source):
        return remote(
            source,
            slot_of(step, part),
            send_sem.at[step, part],
            recv_sem.at[step, part],
            axis,
            right if pieces[part][1] == 0 else left,
        )

    def own_of(step, part):
        which, way, start, _, size = pieces[part]
        shift = 2 * n - 1 - step if way == 0 else 1 + step
        return g_refs[which].at[ring_index((pos + shift) % n, n), :, pl.ds(start, size)]

    for part in range(len(pieces)):
        copy_of(0, part, own_of(0, part)).start()

    def one(step, carry):
        for part in range(len(pieces)):
            slot = slot_of(step - 1, part)
            copy_of(step - 1, part, slot).wait_recv()
            slot[...] = (
                slot[...].astype(jnp.float32) + own_of(step, part)[...].astype(jnp.float32)
            ).astype(held.dtype)
            copy_of(step, part, slot).start()
        return carry

    lax.fori_loop(1, n - 1, one, 0)
    for part, (which, way, start, _, size) in enumerate(pieces):
        slot = slot_of(n - 2, part)
        copy_of(n - 2, part, slot).wait_recv()
        columns = pl.ds(start, size)
        o_refs[which][:, columns] = slot[...].astype(jnp.float32) + g_refs[which][
            me, :, columns
        ].astype(jnp.float32)

    def drain(step, carry):
        for part in range(len(pieces)):
            copy_of(step, part, slot_of(step, part)).wait_send()
        return carry

    lax.fori_loop(0, n - 1, drain, 0)


def ring_sum(gs, plan, axis, ident):
    n, rows, _ = gs[0].shape
    pieces, at = [], 0
    for which, way, start, size in plan:
        pieces.append((which, way, start, at, size))
        at += size
    return pl.pallas_call(
        functools.partial(ring_sum_kernel, n, axis, tuple(pieces), len(gs)),
        out_shape=tuple(jax.ShapeDtypeStruct(g.shape[1:], jnp.float32) for g in gs),
        in_specs=[pl.BlockSpec(memory_space=pltpu.VMEM)] * len(gs),
        out_specs=tuple(pl.BlockSpec(memory_space=pltpu.VMEM) for _ in gs),
        scratch_shapes=[
            pltpu.VMEM((n - 1, rows, at), gs[0].dtype),
            pltpu.SemaphoreType.DMA((n - 1, len(pieces))),
            pltpu.SemaphoreType.DMA((n - 1, len(pieces))),
        ],
        compiler_params=pltpu.CompilerParams(collective_id=ident, has_side_effects=True),
    )(*gs)


def scatter_sum_kernel(axis, x_ref, o_ref, near, far, total, send_sem, recv_sem):
    me, beside, across = quad(axis)
    greet((axis, beside), (axis, across))
    half = o_ref.shape[0] // 2
    parts = [pl.ds(0, half), pl.ds(half, half)]

    def pair(i, k, chunk):
        return remote(
            x_ref.at[chunk, parts[i]],
            near.at[k, parts[i]],
            send_sem.at[i, k],
            recv_sem.at[i, k],
            axis,
            beside,
        )

    copies = [pair(i, 0, (beside + 2) % 4) for i in range(2)]
    copies += [pair(i, 1, beside) for i in range(2)]
    for copy in copies:
        copy.start()
    crossing = []
    for i, rows in enumerate(parts):
        copies[i].wait_recv()
        total[rows] = (
            x_ref[across, rows].astype(jnp.float32) + near[0, rows].astype(jnp.float32)
        ).astype(total.dtype)
        copy = remote(
            total.at[rows], far.at[rows], send_sem.at[i, 2], recv_sem.at[i, 2], axis, across
        )
        copy.start()
        crossing.append(copy)
    for i, rows in enumerate(parts):
        copies[2 + i].wait_recv()
        crossing[i].wait_recv()
        o_ref[rows] = (
            x_ref[me, rows].astype(jnp.float32)
            + near[1, rows].astype(jnp.float32)
            + far[rows].astype(jnp.float32)
        )
    for copy in copies + crossing:
        copy.wait_send()


def scatter_sum(x, axis, ident):
    rows, columns = x.shape[0] // 4, x.shape[1]
    return pl.pallas_call(
        functools.partial(scatter_sum_kernel, axis),
        out_shape=jax.ShapeDtypeStruct((rows, columns), jnp.float32),
        in_specs=[pl.BlockSpec(memory_space=pltpu.VMEM)],
        out_specs=pl.BlockSpec(memory_space=pltpu.VMEM),
        scratch_shapes=[
            pltpu.VMEM((2, rows, columns), x.dtype),
            pltpu.VMEM((rows, columns), x.dtype),
            pltpu.VMEM((rows, columns), x.dtype),
            pltpu.SemaphoreType.DMA((2, 3)),
            pltpu.SemaphoreType.DMA((2, 3)),
        ],
        compiler_params=pltpu.CompilerParams(collective_id=ident, has_side_effects=True),
    )(x.reshape(4, rows, columns))


def chain(decay, state, first, last, backward, ident):
    n = lax.axis_size("shard")
    me = lax.axis_index("shard")
    lines = jnp.zeros((16, DV), jnp.float32)
    lines = lines.at[0, :DK].set(decay).at[1, 0].set(first).at[1, 1].set(last)
    block = jnp.concatenate([state, lines], axis=0).astype(jnp.bfloat16)
    every = ring_gather(block, "shard", ident)
    states = every[:, :DK].astype(jnp.float32)
    decays = every[:, DK, :DK].astype(jnp.float32)
    firsts = every[:, DK + 1, 0].astype(jnp.float32)
    lasts = every[:, DK + 1, 1].astype(jnp.float32)
    place = jnp.arange(n)
    j, i = place[:, None], place[None, :]
    if backward:
        passing = decays
        between = jnp.logical_and(i > me, i < j)
        counted = place > me
    else:
        before = jnp.concatenate([jnp.zeros((1,), jnp.float32), lasts[:-1]])
        passing = decays * (firsts == before).astype(jnp.float32)[:, None]
        between = jnp.logical_and(i > j, i < me)
        counted = place < me
    weight = jnp.prod(jnp.where(between[:, :, None], passing[None], 1.0), axis=1)
    weight = jnp.where(counted[:, None], weight, 0.0)
    incoming = jnp.sum(weight[:, :, None] * states, axis=0)
    prior = jnp.sum(jnp.where(place == me - 1, lasts, 0.0))
    return incoming[None], prior


def rms_scale(values):
    return lax.rsqrt(jnp.mean(values * values, axis=-1, keepdims=True) + EPS)


def group_pass(query, key, value_rows, logdec, segf, state, carry_seg):
    total = query.shape[0]
    heads = query.shape[1]
    count = total // GROUP
    scale = DK ** (-0.5)
    order = jnp.arange(GROUP)
    causal = order[:, None] >= order[None, :]

    def blocks(array):
        return array.reshape((count, GROUP) + array.shape[1:])

    def advance(carry, pieces):
        memory_state, prior = carry
        query_c, key_c, value_segment, decay_c, seg_c = pieces
        cumul = jnp.cumsum(decay_c, axis=0)
        query_decayed = query_c * jnp.exp(cumul) * scale
        key_inc = key_c * jnp.exp(-cumul)
        scores = jnp.einsum("thk,shk->hts", query_decayed, key_inc, precision=HIGH_PRECISION)
        joined = jnp.logical_and(causal, seg_c[:, None] == seg_c[None, :])
        scores = jnp.where(joined[None], scores, 0.0)
        inherit = (seg_c == prior).astype(jnp.float32)
        inside = jnp.einsum("hts,shv->thv", scores, value_segment, precision=HIGH_PRECISION)
        carried_state = jnp.einsum(
            "zsb,sbi->zsi", query_decayed, memory_state, precision=HIGH_PRECISION
        )
        result = inside + inherit[:, None, None] * carried_state
        final_result = cumul[-1]
        keep = (seg_c == seg_c[-1]).astype(jnp.float32)
        key_final_rows = key_c * jnp.exp(final_result[None] - cumul) * keep[:, None, None]
        linked_states = (seg_c[-1] == prior).astype(jnp.float32)
        memory_state = linked_states * jnp.exp(final_result)[
            :, :, None
        ] * memory_state + jnp.einsum(
            "zie,zir->ier", key_final_rows, value_segment, precision=HIGH_PRECISION
        )
        return ((memory_state, seg_c[-1]), result)

    (memory_state, last_seg), outs = lax.scan(
        advance,
        (state, carry_seg),
        (blocks(query), blocks(key), blocks(value_rows), blocks(logdec), blocks(segf)),
        unroll=True,
    )
    return (outs.reshape(total, heads, outs.shape[-1]), memory_state)


def on_device(
    resid_in,
    cotangent,
    segment,
    attn_gain,
    w_query,
    w_key,
    w_value,
    w_outgate,
    w_low,
    w_rank,
    rank_bias,
    head_gain,
    w_out,
    mlp_gain,
    w_gate,
    w_up,
    w_down,
):

    n = lax.axis_size("shard")
    wide = w_gate.shape[1]
    rows = w_query.shape[0]

    def tall(a):
        a = a.reshape(a.shape[0], -1)
        return jnp.pad(a, ((0, rows - a.shape[0]), (0, 0)))

    packed = jnp.concatenate(
        [
            w_query,
            w_key,
            w_value,
            w_outgate,
            w_out.T,
            w_gate,
            w_up,
            w_down.T,
            w_low,
            tall(attn_gain),
            tall(mlp_gain),
            tall(head_gain),
            tall(w_rank[:, 0, :].T),
            tall(rank_bias[0]),
        ],
        axis=1,
    )
    used = packed.shape[1]
    packed = jnp.pad(packed, ((0, 0), (0, -used % LANE)))
    inv_attn = rms_scale(resid_in)
    unit_rows = (resid_in * inv_attn).astype(jnp.bfloat16)
    cot_rows = cotangent.astype(jnp.bfloat16)
    every, both = enter(packed, jnp.concatenate([unit_rows, cot_rows], axis=1), 1)
    spread = every.reshape(n * rows, packed.shape[1])
    edge_out = 2 * DK + 2 * DV
    edge_gate = edge_out + DV
    edge_down = edge_gate + 2 * wide
    edge_low = edge_down + wide
    project_w = spread[:, :edge_out]
    out_wt = spread[:, edge_out:edge_gate]
    gu_w = spread[:, edge_gate:edge_down]
    down_wt = spread[:, edge_down:edge_low]
    tail = every[:, :, edge_low:]
    low_w = tail[:, :, :GATE_RANK].reshape(D, GATE_RANK)
    gain_attn = tail[:, :, GATE_RANK].reshape(D).astype(jnp.float32)
    gain_mlp = tail[:, :, GATE_RANK + 1].reshape(D).astype(jnp.float32)
    gain_head = tail[:, : DV // n, GATE_RANK + 2].reshape(DV).astype(jnp.float32)
    rank_w = tail[:, : DK // n, GATE_RANK + 3 : 2 * GATE_RANK + 3].reshape(DK, GATE_RANK).T
    bias_w = tail[:, : DK // n, 2 * GATE_RANK + 3].reshape(DK)
    length = segment.shape[0]
    local_heads = 1
    scale = DK ** (-0.5)
    normed_in = (
        (both[:, :, :D].astype(jnp.float32) * gain_attn).astype(jnp.bfloat16).reshape(length, D)
    )
    cot_bf = both[:, :, D:].reshape(length, D)
    projected = jnp.dot(normed_in, project_w, preferred_element_type=jnp.float32)
    query = projected[:, :DK].reshape(length, local_heads, DK)
    key = projected[:, DK : 2 * DK].reshape(length, local_heads, DK)
    value_rows = projected[:, 2 * DK : 2 * DK + DV].reshape(length, local_heads, DV)
    outgate = projected[:, 2 * DK + DV :].reshape(length, local_heads, DV)
    low = jnp.dot(normed_in, low_w, preferred_element_type=jnp.float32)
    rank_mat = rank_w.astype(jnp.float32).reshape(GATE_RANK, local_heads * DK)
    logit = jnp.dot(low, rank_mat, precision=HIGH_PRECISION) + bias_w.astype(jnp.float32).reshape(
        local_heads * DK
    )
    logdec = (jax.nn.log_sigmoid(logit) / 16.0).reshape(length, local_heads, DK)
    segf = segment.astype(jnp.float32) + 1.0
    first_seg = segf[:1]
    last_seg = segf[-1:]
    cumul = jnp.cumsum(logdec, axis=0)
    keep = (segf == last_seg[0]).astype(jnp.float32)
    key_final_rows = key * jnp.exp(cumul[-1][None] - cumul) * keep[:, None, None]
    summary_state = jnp.einsum("zie,zir->ier", key_final_rows, value_rows, precision=HIGH_PRECISION)
    through = jnp.exp(cumul[-1]) * (first_seg[0] == last_seg[0]).astype(jnp.float32)
    state_in, prior = chain(through[0], summary_state[0], first_seg[0], last_seg[0], False, 3)

    def mixer(query_in, key_in, value_in, decay_in):
        return group_pass(query_in, key_in, value_in, decay_in, segf, state_in, prior)

    (mixed, state_out), mixer_back = jax.vjp(mixer, query, key, value_rows, logdec)
    inv_head = rms_scale(mixed)
    headnormed = mixed * inv_head * gain_head
    sigma_out = jax.nn.sigmoid(outgate)
    swish_out = outgate * sigma_out
    gated = (headnormed * swish_out).reshape(length, local_heads * DV).astype(jnp.bfloat16)
    resid_mid = resid_in + scatter_sum(
        jnp.dot(gated, out_wt.T, preferred_element_type=jnp.float32).astype(jnp.bfloat16),
        "head",
        4,
    )
    inv_mlp = rms_scale(resid_mid)
    mid_rows = (resid_mid * inv_mlp * gain_mlp).astype(jnp.bfloat16)
    normed_mid = gather(mid_rows, "head", 5).reshape(length, D)
    gate_up = jnp.dot(normed_mid, gu_w, preferred_element_type=jnp.float32)
    gate_pre = gate_up[:, :wide]
    up_pre = gate_up[:, wide:]
    sigma_gate = jax.nn.sigmoid(gate_pre)
    active = gate_pre * sigma_gate
    hidden = (active * up_pre).astype(jnp.bfloat16)
    d_hidden = jnp.dot(cot_bf, down_wt, preferred_element_type=jnp.float32)
    d_gatepre = (d_hidden * up_pre * sigma_gate * (1.0 + gate_pre * (1.0 - sigma_gate))).astype(
        jnp.bfloat16
    )
    d_uppre = (d_hidden * active).astype(jnp.bfloat16)
    d_gu = jnp.concatenate([d_gatepre, d_uppre], axis=1)
    grad_down = jnp.dot(cot_bf.T, hidden, preferred_element_type=jnp.float32)
    grad_gu = jnp.dot(normed_mid.T, d_gu, preferred_element_type=jnp.float32)
    shares = jnp.concatenate(
        [
            jnp.dot(hidden, down_wt.T, preferred_element_type=jnp.float32).astype(jnp.bfloat16),
            jnp.dot(d_gu, gu_w.T, preferred_element_type=jnp.float32).astype(jnp.bfloat16),
        ],
        axis=1,
    )
    summed = scatter_sum(shares, "head", 6)
    resid_out = resid_mid + summed[:, :D]
    d_normmid = summed[:, D:]
    part_mlp_gain = jnp.sum(d_normmid * resid_mid * inv_mlp, axis=0)
    scaled_mid = gain_mlp * d_normmid
    d_mid = (
        cotangent
        + inv_mlp * scaled_mid
        - resid_mid * inv_mlp**3 * jnp.mean(scaled_mid * resid_mid, axis=-1, keepdims=True)
    )
    dmid_rows = d_mid.astype(jnp.bfloat16)
    dmid_bf = gather(dmid_rows, "head", 7).reshape(length, D)
    d_gated = jnp.dot(dmid_bf, out_wt, preferred_element_type=jnp.float32).reshape(
        length, local_heads, DV
    )
    grad_out = jnp.dot(dmid_bf.T, gated, preferred_element_type=jnp.float32)
    d_head = d_gated * swish_out
    d_outgate = (
        (d_gated * headnormed * sigma_out * (1.0 + outgate * (1.0 - sigma_out)))
        .reshape(length, local_heads * DV)
        .astype(jnp.bfloat16)
    )
    part_head_gain = jnp.sum(d_head * mixed * inv_head, axis=(0, 1))
    scaled_head = gain_head * d_head
    mixed_gradient = inv_head * scaled_head - mixed * inv_head**3 * jnp.mean(
        scaled_head * mixed, axis=-1, keepdims=True
    )
    inherit = (segf == prior).astype(jnp.float32)
    weighted_query = query * jnp.exp(cumul) * inherit[:, None, None] * scale
    local_gradient = jnp.einsum(
        "zie,zir->ier", weighted_query, mixed_gradient, precision=HIGH_PRECISION
    )
    through_all = jnp.exp(cumul[-1]) * (last_seg[0] == prior).astype(jnp.float32)
    nothing = jnp.zeros((), jnp.float32)
    outgoing, _ = chain(through_all[0], local_gradient[0], nothing, nothing, True, 8)
    d_query, d_key, d_value, d_logdec = mixer_back((mixed_gradient, outgoing))
    query_bf = d_query.reshape(length, local_heads * DK).astype(jnp.bfloat16)
    key_bf = d_key.reshape(length, local_heads * DK).astype(jnp.bfloat16)
    value_bf = d_value.reshape(length, local_heads * DV).astype(jnp.bfloat16)
    d_logit = d_logdec.reshape(length, local_heads * DK) * jax.nn.sigmoid(-logit) / 16.0
    grad_bias = jnp.sum(d_logit, axis=0).reshape(local_heads, DK)
    grad_rank = jnp.dot(low.T, d_logit, precision=HIGH_PRECISION).reshape(
        GATE_RANK, local_heads, DK
    )
    d_low = (
        jnp.einsum(
            "thk,rhk->thr",
            d_logit.reshape(length, local_heads, DK),
            rank_w.astype(jnp.float32).reshape(GATE_RANK, local_heads, DK),
            precision=HIGH_PRECISION,
        )
        .astype(jnp.bfloat16)
        .reshape(length, local_heads * GATE_RANK)
    )
    part_low = (
        jnp.dot(normed_in.T, d_low, preferred_element_type=jnp.float32)
        .reshape(D, local_heads, GATE_RANK)
        .sum(axis=1)
    )
    d_project = jnp.concatenate([query_bf, key_bf, value_bf, d_outgate], axis=1)
    grad_project = jnp.dot(normed_in.T, d_project, preferred_element_type=jnp.float32)
    low_rows = low_w.T
    total_term = jnp.dot(d_project, project_w.T, preferred_element_type=jnp.float32)
    d_normin = scatter_sum(
        (total_term + jnp.dot(d_low, low_rows, preferred_element_type=jnp.float32)).astype(
            jnp.bfloat16
        ),
        "head",
        9,
    )
    part_attn_gain = jnp.sum(d_normin * resid_in * inv_attn, axis=0)
    scaled_in = gain_attn * d_normin
    grad_in = (
        d_mid
        + inv_attn * scaled_in
        - resid_in * inv_attn**3 * jnp.mean(scaled_in * resid_in, axis=-1, keepdims=True)
    )

    def owners(a):
        a = a.reshape(n, a.shape[0] // n, -1)
        return jnp.pad(a, ((0, 0), (0, rows - a.shape[1]), (0, 0))).reshape(D, -1)

    lean = jnp.concatenate(
        [
            part_low,
            part_attn_gain[:, None],
            part_mlp_gain[:, None],
            owners(part_head_gain),
            owners(grad_rank[:, 0, :].T),
            owners(grad_bias[0]),
        ],
        axis=1,
    )
    lean = jnp.pad(lean, ((0, 0), (0, packed.shape[1] - used)))
    grads = [
        g.astype(jnp.bfloat16).reshape(n, rows, -1)
        for g in (
            grad_project,
            grad_out,
            grad_gu,
            jnp.concatenate([grad_down, lean], axis=1),
        )
    ]
    middle = (wide // LANE + 1) * LANE
    plan = (
        (2, 0, 0, middle),
        (3, 1, 0, grads[3].shape[2]),
        (0, 0, 0, edge_out),
        (2, 1, middle, 2 * wide - middle),
        (1, 1, 0, DV),
    )
    own_project, own_out, own_gu, own_rest = ring_sum(grads, plan, "shard", 10)
    heads = lax.axis_size("head")
    shared = own_rest[:, wide : wide + GATE_RANK + 3]
    gain_rows = DV // n
    final_rank = own_rest[: DK // n, wide + GATE_RANK + 3 : wide + 2 * GATE_RANK + 3]
    final_bias = own_rest[: DK // n, wide + 2 * GATE_RANK + 3]
    shares = jnp.concatenate(
        [
            shared[:, : GATE_RANK + 2].reshape(heads, rows // heads, GATE_RANK + 2),
            jnp.pad(
                shared[:gain_rows, GATE_RANK + 2].reshape(heads, gain_rows // heads, 1),
                ((0, 0), (0, (rows - gain_rows) // heads), (0, 0)),
            ),
        ],
        axis=2,
    )
    deep = max(rows // heads, 32)
    shares = jnp.pad(
        shares, ((0, 0), (0, deep - rows // heads), (0, LANE - GATE_RANK - 3))
    ).reshape(heads * deep, LANE)
    final = scatter_sum(shares.astype(jnp.bfloat16), "head", 11)[: rows // heads]
    return (
        resid_out,
        grad_in,
        final[:, GATE_RANK],
        own_project[:, :DK],
        own_project[:, DK : 2 * DK],
        own_project[:, 2 * DK : 2 * DK + DV],
        own_project[:, 2 * DK + DV :],
        final[:, :GATE_RANK],
        final_rank.T.reshape(GATE_RANK, 1, DK // n),
        final_bias.reshape(1, DK // n),
        final[: gain_rows // heads, GATE_RANK + 2],
        own_out.T,
        final[:, GATE_RANK + 1],
        own_gu[:, :wide],
        own_gu[:, wide:],
        own_rest[:, :wide].T,
    )


def solution(mesh):
    in_specs = (
        P(("shard", "head"), None),
        P(("shard", "head"), None),
        P("shard"),
        P("shard"),
        P("shard", "head"),
        P("shard", "head"),
        P("shard", "head"),
        P("shard", "head"),
        P("shard", None),
        P(None, "head", "shard"),
        P("head", "shard"),
        P("shard"),
        P("head", "shard"),
        P("shard"),
        P("shard", "head"),
        P("shard", "head"),
        P("head", "shard"),
    )
    out_specs = (
        P(("shard", "head"), None),
        P(("shard", "head"), None),
        P(("shard", "head")),
        P("shard", "head"),
        P("shard", "head"),
        P("shard", "head"),
        P("shard", "head"),
        P(("shard", "head"), None),
        P(None, "head", "shard"),
        P("head", "shard"),
        P(("shard", "head")),
        P("head", "shard"),
        P(("shard", "head")),
        P("shard", "head"),
        P("shard", "head"),
        P("head", "shard"),
    )
    return jax.shard_map(
        on_device, mesh=mesh, in_specs=in_specs, out_specs=out_specs, check_vma=False
    )
```

```python
import functools

import jax
import jax.numpy as jnp
from jax import lax
from jax.experimental import pallas as pl
from jax.experimental.pallas import tpu as pltpu
from jax.sharding import PartitionSpec as P

D = 1024
DK = 128
DV = 256
GATE_RANK = 16
GROUP = 64
LANE = 128
MESH = pl.DeviceIdType.MESH


EPS = 1e-06
HIGH_PRECISION = lax.Precision.HIGHEST


def ring_index(pos, n):
    return jnp.where(pos < n // 2, 2 * pos, 2 * (n - 1 - pos) + 1)


def ring_place(index, n):
    return jnp.where(index % 2 == 0, index // 2, n - 1 - index // 2)


def greet(*pairs):
    barrier = pltpu.get_barrier_semaphore()
    for axis, peer in pairs:
        pl.semaphore_signal(barrier, inc=1, device_id={axis: peer}, device_id_type=MESH)
    pl.semaphore_wait(barrier, len(pairs))


def remote(source, target, send_sem, recv_sem, axis, peer):
    return pltpu.make_async_remote_copy(
        src_ref=source,
        dst_ref=target,
        send_sem=send_sem,
        recv_sem=recv_sem,
        device_id={axis: peer},
        device_id_type=MESH,
    )


def quad(axis):
    me = lax.axis_index(axis)
    return me, me + 1 - 2 * (me % 2), (me + 2) % 4


def cuts(columns, parts):
    lanes = columns // LANE
    sizes = [(lanes // parts + (1 if i < lanes % parts else 0)) * LANE for i in range(parts)]
    starts = [sum(sizes[:i]) for i in range(parts)]
    return list(zip(starts, sizes))


def ring_gather_kernel(n, axis, x_ref, o_ref, own_sem, send_sem, recv_sem):
    right, left = ring_sides(n, axis)
    greet((axis, left), (axis, right))
    ring_gather_body(n, axis, x_ref, o_ref, own_sem, send_sem, recv_sem, None)


def ring_sides(n, axis):
    pos = ring_place(lax.axis_index(axis), n)
    return ring_index((pos + 1) % n, n), ring_index((pos + n - 1) % n, n)


def ring_gather_body(n, axis, x_ref, o_ref, own_sem, send_sem, recv_sem, meanwhile):
    me = lax.axis_index(axis)
    pos = ring_place(me, n)
    right, left = ring_sides(n, axis)
    own = pltpu.make_async_copy(x_ref, o_ref.at[me], own_sem)
    own.start()
    pieces = cuts(x_ref.shape[1], 2)
    steps = n // 2
    sent = {}
    for step in range(steps):
        for part, (start, size) in enumerate(pieces):
            for way in range(2):
                if step == steps - 1 and part != way:
                    continue
                shift = n - step if way == 0 else step
                block = ring_index((pos + shift) % n, n)
                columns = pl.ds(start, size)
                if step > 0:
                    sent[(step - 1, part, way)].wait_recv()
                source = x_ref.at[:, columns] if step == 0 else o_ref.at[block, :, columns]
                copy = pltpu.make_async_remote_copy(
                    src_ref=source,
                    dst_ref=o_ref.at[block, :, columns],
                    send_sem=send_sem.at[step, part, way],
                    recv_sem=recv_sem.at[step, part, way],
                    device_id={axis: right if way == 0 else left},
                    device_id_type=MESH,
                )
                copy.start()
                sent[(step, part, way)] = copy
        if step == 0 and meanwhile is not None:
            meanwhile()
    for (step, part, way), copy in sent.items():
        if (step + 1, part, way) not in sent:
            copy.wait_recv()
    for copy in sent.values():
        copy.wait_send()
    own.wait()


def ring_gather(x, axis, ident):
    n = lax.axis_size(axis)
    return pl.pallas_call(
        functools.partial(ring_gather_kernel, n, axis),
        out_shape=jax.ShapeDtypeStruct((n,) + x.shape, x.dtype),
        in_specs=[pl.BlockSpec(memory_space=pltpu.VMEM)],
        out_specs=pl.BlockSpec(memory_space=pl.ANY),
        scratch_shapes=[
            pltpu.SemaphoreType.DMA,
            pltpu.SemaphoreType.DMA((n // 2, 2, 2)),
            pltpu.SemaphoreType.DMA((n // 2, 2, 2)),
        ],
        compiler_params=pltpu.CompilerParams(collective_id=ident, has_side_effects=True),
    )(x)


def quad_gather_parts(axis, x_ref, o_ref, send_sem, recv_sem):
    me, beside, across = quad(axis)
    half = x_ref.shape[0] // 2
    parts = [pl.ds(0, half), pl.ds(half, half)]
    first = [
        (
            remote(x_ref.at[rows], o_ref.at[me, rows], send_sem.at[i, 0], recv_sem.at[i, 0], axis, across),
            remote(x_ref.at[rows], o_ref.at[me, rows], send_sem.at[i, 1], recv_sem.at[i, 1], axis, beside),
        )
        for i, rows in enumerate(parts)
    ]
    onward = [
        remote(
            o_ref.at[across, rows],
            o_ref.at[across, rows],
            send_sem.at[i, 2],
            recv_sem.at[i, 2],
            axis,
            beside,
        )
        for i, rows in enumerate(parts)
    ]

    def start():
        for far, near in first:
            far.start()
            near.start()
        o_ref[me] = x_ref[...]

    def relay():
        for (far, _), more in zip(first, onward):
            far.wait_recv()
            more.start()

    def finish():
        for (far, near), more in zip(first, onward):
            near.wait_recv()
            more.wait_recv()
            far.wait_send()
            near.wait_send()
            more.wait_send()

    return start, relay, finish


def gather_kernel(axis, x_ref, o_ref, send_sem, recv_sem):
    _, beside, across = quad(axis)
    greet((axis, beside), (axis, across))
    start, relay, finish = quad_gather_parts(axis, x_ref, o_ref, send_sem, recv_sem)
    start()
    relay()
    finish()


def gather(x, axis, ident):
    return pl.pallas_call(
        functools.partial(gather_kernel, axis),
        out_shape=jax.ShapeDtypeStruct((4,) + x.shape, x.dtype),
        in_specs=[pl.BlockSpec(memory_space=pltpu.VMEM)],
        out_specs=pl.BlockSpec(memory_space=pltpu.VMEM),
        scratch_shapes=[
            pltpu.SemaphoreType.DMA((2, 3)),
            pltpu.SemaphoreType.DMA((2, 3)),
        ],
        compiler_params=pltpu.CompilerParams(collective_id=ident, has_side_effects=True),
    )(x)


def enter_kernel(n, w_ref, x_ref, spread_ref, o_ref, own_sem, send_w, recv_w, send_x, recv_x):
    right, left = ring_sides(n, "shard")
    _, beside, across = quad("head")
    greet(("shard", left), ("shard", right), ("head", beside), ("head", across))
    start, relay, finish = quad_gather_parts("head", x_ref, o_ref, send_x, recv_x)
    start()
    ring_gather_body(n, "shard", w_ref, spread_ref, own_sem, send_w, recv_w, relay)
    finish()


def enter(weights, x, ident):
    n = lax.axis_size("shard")
    return pl.pallas_call(
        functools.partial(enter_kernel, n),
        out_shape=(
            jax.ShapeDtypeStruct((n,) + weights.shape, weights.dtype),
            jax.ShapeDtypeStruct((4,) + x.shape, x.dtype),
        ),
        in_specs=[pl.BlockSpec(memory_space=pltpu.VMEM)] * 2,
        out_specs=(
            pl.BlockSpec(memory_space=pl.ANY),
            pl.BlockSpec(memory_space=pltpu.VMEM),
        ),
        scratch_shapes=[
            pltpu.SemaphoreType.DMA,
            pltpu.SemaphoreType.DMA((n // 2, 2, 2)),
            pltpu.SemaphoreType.DMA((n // 2, 2, 2)),
            pltpu.SemaphoreType.DMA((2, 3)),
            pltpu.SemaphoreType.DMA((2, 3)),
        ],
        compiler_params=pltpu.CompilerParams(collective_id=ident, has_side_effects=True),
    )(weights, x)


def ring_sum_kernel(n, axis, pieces, count, *refs):
    g_refs, o_refs = refs[:count], refs[count : 2 * count]
    held, send_sem, recv_sem = refs[2 * count :]
    me = lax.axis_index(axis)
    pos = ring_place(me, n)
    right, left = ring_sides(n, axis)
    greet((axis, left), (axis, right))

    def slot_of(step, part):
        start, size = pieces[part][3:]
        return held.at[step, :, pl.ds(start, size)]

    def copy_of(step, part, source):
        return remote(
            source,
            slot_of(step, part),
            send_sem.at[step, part],
            recv_sem.at[step, part],
            axis,
            right if pieces[part][1] == 0 else left,
        )

    def own_of(step, part):
        which, way, start, _, size = pieces[part]
        shift = 2 * n - 1 - step if way == 0 else 1 + step
        return g_refs[which].at[ring_index((pos + shift) % n, n), :, pl.ds(start, size)]

    for part in range(len(pieces)):
        copy_of(0, part, own_of(0, part)).start()

    def one(step, carry):
        for part in range(len(pieces)):
            slot = slot_of(step - 1, part)
            copy_of(step - 1, part, slot).wait_recv()
            slot[...] = (
                slot[...].astype(jnp.float32) + own_of(step, part)[...].astype(jnp.float32)
            ).astype(held.dtype)
            copy_of(step, part, slot).start()
        return carry

    lax.fori_loop(1, n - 1, one, 0)
    for part, (which, way, start, _, size) in enumerate(pieces):
        slot = slot_of(n - 2, part)
        copy_of(n - 2, part, slot).wait_recv()
        columns = pl.ds(start, size)
        o_refs[which][:, columns] = slot[...].astype(jnp.float32) + g_refs[which][
            me, :, columns
        ].astype(jnp.float32)

    def drain(step, carry):
        for part in range(len(pieces)):
            copy_of(step, part, slot_of(step, part)).wait_send()
        return carry

    lax.fori_loop(0, n - 1, drain, 0)


def ring_sum(gs, plan, axis, ident):
    n, rows, _ = gs[0].shape
    pieces, at = [], 0
    for which, way, start, size in plan:
        pieces.append((which, way, start, at, size))
        at += size
    return pl.pallas_call(
        functools.partial(ring_sum_kernel, n, axis, tuple(pieces), len(gs)),
        out_shape=tuple(jax.ShapeDtypeStruct(g.shape[1:], jnp.float32) for g in gs),
        in_specs=[pl.BlockSpec(memory_space=pltpu.VMEM)] * len(gs),
        out_specs=tuple(pl.BlockSpec(memory_space=pltpu.VMEM) for _ in gs),
        scratch_shapes=[
            pltpu.VMEM((n - 1, rows, at), gs[0].dtype),
            pltpu.SemaphoreType.DMA((n - 1, len(pieces))),
            pltpu.SemaphoreType.DMA((n - 1, len(pieces))),
        ],
        compiler_params=pltpu.CompilerParams(collective_id=ident, has_side_effects=True),
    )(*gs)


def scatter_sum_kernel(axis, x_ref, o_ref, near, far, total, send_sem, recv_sem):
    me, beside, across = quad(axis)
    greet((axis, beside), (axis, across))
    half = o_ref.shape[0] // 2
    parts = [pl.ds(0, half), pl.ds(half, half)]

    def pair(i, k, chunk):
        return remote(
            x_ref.at[chunk, parts[i]],
            near.at[k, parts[i]],
            send_sem.at[i, k],
            recv_sem.at[i, k],
            axis,
            beside,
        )

    copies = [pair(i, 0, (beside + 2) % 4) for i in range(2)]
    copies += [pair(i, 1, beside) for i in range(2)]
    for copy in copies:
        copy.start()
    crossing = []
    for i, rows in enumerate(parts):
        copies[i].wait_recv()
        total[rows] = (
            x_ref[across, rows].astype(jnp.float32) + near[0, rows].astype(jnp.float32)
        ).astype(total.dtype)
        copy = remote(
            total.at[rows], far.at[rows], send_sem.at[i, 2], recv_sem.at[i, 2], axis, across
        )
        copy.start()
        crossing.append(copy)
    for i, rows in enumerate(parts):
        copies[2 + i].wait_recv()
        crossing[i].wait_recv()
        o_ref[rows] = (
            x_ref[me, rows].astype(jnp.float32)
            + near[1, rows].astype(jnp.float32)
            + far[rows].astype(jnp.float32)
        )
    for copy in copies + crossing:
        copy.wait_send()


def scatter_sum(x, axis, ident):
    rows, columns = x.shape[0] // 4, x.shape[1]
    return pl.pallas_call(
        functools.partial(scatter_sum_kernel, axis),
        out_shape=jax.ShapeDtypeStruct((rows, columns), jnp.float32),
        in_specs=[pl.BlockSpec(memory_space=pltpu.VMEM)],
        out_specs=pl.BlockSpec(memory_space=pltpu.VMEM),
        scratch_shapes=[
            pltpu.VMEM((2, rows, columns), x.dtype),
            pltpu.VMEM((rows, columns), x.dtype),
            pltpu.VMEM((rows, columns), x.dtype),
            pltpu.SemaphoreType.DMA((2, 3)),
            pltpu.SemaphoreType.DMA((2, 3)),
        ],
        compiler_params=pltpu.CompilerParams(collective_id=ident, has_side_effects=True),
    )(x.reshape(4, rows, columns))


def chain(decay, state, first, last, backward, ident):
    n = lax.axis_size("shard")
    me = lax.axis_index("shard")
    lines = jnp.zeros((16, DV), jnp.float32)
    lines = lines.at[0, :DK].set(decay).at[1, 0].set(first).at[1, 1].set(last)
    block = jnp.concatenate([state, lines], axis=0).astype(jnp.bfloat16)
    every = ring_gather(block, "shard", ident)
    states = every[:, :DK].astype(jnp.float32)
    decays = every[:, DK, :DK].astype(jnp.float32)
    firsts = every[:, DK + 1, 0].astype(jnp.float32)
    lasts = every[:, DK + 1, 1].astype(jnp.float32)
    place = jnp.arange(n)
    j, i = place[:, None], place[None, :]
    if backward:
        passing = decays
        between = jnp.logical_and(i > me, i < j)
        counted = place > me
    else:
        before = jnp.concatenate([jnp.zeros((1,), jnp.float32), lasts[:-1]])
        passing = decays * (firsts == before).astype(jnp.float32)[:, None]
        between = jnp.logical_and(i > j, i < me)
        counted = place < me
    weight = jnp.prod(jnp.where(between[:, :, None], passing[None], 1.0), axis=1)
    weight = jnp.where(counted[:, None], weight, 0.0)
    incoming = jnp.sum(weight[:, :, None] * states, axis=0)
    prior = jnp.sum(jnp.where(place == me - 1, lasts, 0.0))
    return incoming[None], prior


def rms_scale(values):
    return lax.rsqrt(jnp.mean(values * values, axis=-1, keepdims=True) + EPS)


def group_pass(query, key, value_rows, logdec, segf, state, carry_seg):
    total = query.shape[0]
    heads = query.shape[1]
    count = total // GROUP
    scale = DK ** (-0.5)
    order = jnp.arange(GROUP)
    causal = order[:, None] >= order[None, :]

    def blocks(array):
        return array.reshape((count, GROUP) + array.shape[1:])

    def advance(carry, pieces):
        memory_state, prior = carry
        query_c, key_c, value_segment, decay_c, seg_c = pieces
        cumul = jnp.cumsum(decay_c, axis=0)
        query_decayed = query_c * jnp.exp(cumul) * scale
        key_inc = key_c * jnp.exp(-cumul)
        scores = jnp.einsum("thk,shk->hts", query_decayed, key_inc, precision=HIGH_PRECISION)
        joined = jnp.logical_and(causal, seg_c[:, None] == seg_c[None, :])
        scores = jnp.where(joined[None], scores, 0.0)
        inherit = (seg_c == prior).astype(jnp.float32)
        inside = jnp.einsum("hts,shv->thv", scores, value_segment, precision=HIGH_PRECISION)
        carried_state = jnp.einsum(
            "zsb,sbi->zsi", query_decayed, memory_state, precision=HIGH_PRECISION
        )
        result = inside + inherit[:, None, None] * carried_state
        final_result = cumul[-1]
        keep = (seg_c == seg_c[-1]).astype(jnp.float32)
        key_final_rows = key_c * jnp.exp(final_result[None] - cumul) * keep[:, None, None]
        linked_states = (seg_c[-1] == prior).astype(jnp.float32)
        memory_state = linked_states * jnp.exp(final_result)[
            :, :, None
        ] * memory_state + jnp.einsum(
            "zie,zir->ier", key_final_rows, value_segment, precision=HIGH_PRECISION
        )
        return ((memory_state, seg_c[-1]), result)

    (memory_state, last_seg), outs = lax.scan(
        advance,
        (state, carry_seg),
        (blocks(query), blocks(key), blocks(value_rows), blocks(logdec), blocks(segf)),
        unroll=True,
    )
    return (outs.reshape(total, heads, outs.shape[-1]), memory_state)


def on_device(
    resid_in,
    cotangent,
    segment,
    attn_gain,
    w_query,
    w_key,
    w_value,
    w_outgate,
    w_low,
    w_rank,
    rank_bias,
    head_gain,
    w_out,
    mlp_gain,
    w_gate,
    w_up,
    w_down,
):

    n = lax.axis_size("shard")
    wide = w_gate.shape[1]
    rows = w_query.shape[0]

    def line(a):
        return jnp.pad(a, (0, LANE - a.shape[0]))[None]

    def filled(a, height, width):
        return jnp.pad(a, ((0, height - a.shape[0]), (0, width - a.shape[1])))

    spare = -(3 * wide + GATE_RANK) % LANE
    lines = jnp.concatenate(
        [line(attn_gain), line(mlp_gain), line(head_gain), line(rank_bias[0])], axis=0
    )
    packed = jnp.concatenate(
        [
            w_query,
            w_key,
            w_value,
            w_outgate,
            w_out.T,
            w_gate,
            w_up,
            w_down.T,
            w_low,
            filled(w_rank[:, 0, :], rows, spare),
            filled(lines, rows, LANE),
        ],
        axis=1,
    )
    inv_attn = rms_scale(resid_in)
    unit_rows = resid_in * inv_attn
    every, both = enter(packed, jnp.concatenate([unit_rows, cotangent], axis=1), 1)
    spread = every.reshape(n * rows, packed.shape[1])
    edge_out = 2 * DK + 2 * DV
    edge_gate = edge_out + DV
    edge_down = edge_gate + 2 * wide
    edge_low = edge_down + wide
    project_w = spread[:, :edge_out]
    out_wt = spread[:, edge_out:edge_gate]
    gu_w = spread[:, edge_gate:edge_down]
    down_wt = spread[:, edge_down:edge_low]
    tail = every[:, :, edge_low : edge_low + GATE_RANK + spare]
    vectors = every[:, :4, edge_low + GATE_RANK + spare :]
    low_w = tail[:, :, :GATE_RANK].reshape(D, GATE_RANK)
    gain_attn = vectors[:, 0, :rows].reshape(D).astype(jnp.float32)
    gain_mlp = vectors[:, 1, :rows].reshape(D).astype(jnp.float32)
    gain_head = vectors[:, 2, : DV // n].reshape(DV).astype(jnp.float32)
    bias_w = vectors[:, 3, : DK // n].reshape(DK)
    rank_w = (
        tail[:, :GATE_RANK, GATE_RANK : GATE_RANK + DK // n]
        .transpose(1, 0, 2)
        .reshape(GATE_RANK, DK)
    )
    length = segment.shape[0]
    local_heads = 1
    scale = DK ** (-0.5)
    normed_in = (
        (both[:, :, :D] * gain_attn).astype(jnp.bfloat16).reshape(length, D)
    )
    cot_bf = both[:, :, D:].reshape(length, D).astype(jnp.bfloat16)
    projected = jnp.dot(normed_in, project_w, preferred_element_type=jnp.float32)
    query = projected[:, :DK].reshape(length, local_heads, DK)
    key = projected[:, DK : 2 * DK].reshape(length, local_heads, DK)
    value_rows = projected[:, 2 * DK : 2 * DK + DV].reshape(length, local_heads, DV)
    outgate = projected[:, 2 * DK + DV :].reshape(length, local_heads, DV)
    low = jnp.dot(normed_in, low_w, preferred_element_type=jnp.float32)
    rank_mat = rank_w.astype(jnp.float32).reshape(GATE_RANK, local_heads * DK)
    logit = jnp.dot(low, rank_mat, precision=HIGH_PRECISION) + bias_w.astype(jnp.float32).reshape(
        local_heads * DK
    )
    logdec = (jax.nn.log_sigmoid(logit) / 16.0).reshape(length, local_heads, DK)
    segf = segment.astype(jnp.float32) + 1.0
    first_seg = segf[:1]
    last_seg = segf[-1:]
    cumul = jnp.cumsum(logdec, axis=0)
    keep = (segf == last_seg[0]).astype(jnp.float32)
    key_final_rows = key * jnp.exp(cumul[-1][None] - cumul) * keep[:, None, None]
    summary_state = jnp.einsum("zie,zir->ier", key_final_rows, value_rows, precision=HIGH_PRECISION)
    through = jnp.exp(cumul[-1]) * (first_seg[0] == last_seg[0]).astype(jnp.float32)
    state_in, prior = chain(through[0], summary_state[0], first_seg[0], last_seg[0], False, 3)

    def mixer(query_in, key_in, value_in, decay_in):
        return group_pass(query_in, key_in, value_in, decay_in, segf, state_in, prior)

    (mixed, state_out), mixer_back = jax.vjp(mixer, query, key, value_rows, logdec)
    inv_head = rms_scale(mixed)
    headnormed = mixed * inv_head * gain_head
    sigma_out = jax.nn.sigmoid(outgate)
    swish_out = outgate * sigma_out
    gated = (headnormed * swish_out).reshape(length, local_heads * DV).astype(jnp.bfloat16)
    resid_mid = resid_in + scatter_sum(
        jnp.dot(gated, out_wt.T, preferred_element_type=jnp.float32).astype(jnp.bfloat16),
        "head",
        4,
    )
    inv_mlp = rms_scale(resid_mid)
    mid_rows = (resid_mid * inv_mlp * gain_mlp).astype(jnp.bfloat16)
    normed_mid = gather(mid_rows, "head", 5).reshape(length, D)
    gate_up = jnp.dot(normed_mid, gu_w, preferred_element_type=jnp.float32)
    gate_pre = gate_up[:, :wide]
    up_pre = gate_up[:, wide:]
    sigma_gate = jax.nn.sigmoid(gate_pre)
    active = gate_pre * sigma_gate
    hidden = (active * up_pre).astype(jnp.bfloat16)
    d_hidden = jnp.dot(cot_bf, down_wt, preferred_element_type=jnp.float32)
    d_gatepre = (d_hidden * up_pre * sigma_gate * (1.0 + gate_pre * (1.0 - sigma_gate))).astype(
        jnp.bfloat16
    )
    d_uppre = (d_hidden * active).astype(jnp.bfloat16)
    d_gu = jnp.concatenate([d_gatepre, d_uppre], axis=1)
    grad_down = jnp.dot(cot_bf.T, hidden, preferred_element_type=jnp.float32)
    grad_gu = jnp.dot(normed_mid.T, d_gu, preferred_element_type=jnp.float32)
    shares = jnp.concatenate(
        [
            jnp.dot(hidden, down_wt.T, preferred_element_type=jnp.float32).astype(jnp.bfloat16),
            jnp.dot(d_gu, gu_w.T, preferred_element_type=jnp.float32).astype(jnp.bfloat16),
        ],
        axis=1,
    )
    summed = scatter_sum(shares, "head", 6)
    resid_out = resid_mid + summed[:, :D]
    d_normmid = summed[:, D:]
    part_mlp_gain = jnp.sum(d_normmid * resid_mid * inv_mlp, axis=0)
    scaled_mid = gain_mlp * d_normmid
    d_mid = (
        cotangent
        + inv_mlp * scaled_mid
        - resid_mid * inv_mlp**3 * jnp.mean(scaled_mid * resid_mid, axis=-1, keepdims=True)
    )
    dmid_rows = d_mid.astype(jnp.bfloat16)
    dmid_bf = gather(dmid_rows, "head", 7).reshape(length, D)
    d_gated = jnp.dot(dmid_bf, out_wt, preferred_element_type=jnp.float32).reshape(
        length, local_heads, DV
    )
    grad_out = jnp.dot(dmid_bf.T, gated, preferred_element_type=jnp.float32)
    d_head = d_gated * swish_out
    d_outgate = (
        (d_gated * headnormed * sigma_out * (1.0 + outgate * (1.0 - sigma_out)))
        .reshape(length, local_heads * DV)
        .astype(jnp.bfloat16)
    )
    part_head_gain = jnp.sum(d_head * mixed * inv_head, axis=(0, 1))
    scaled_head = gain_head * d_head
    mixed_gradient = inv_head * scaled_head - mixed * inv_head**3 * jnp.mean(
        scaled_head * mixed, axis=-1, keepdims=True
    )
    inherit = (segf == prior).astype(jnp.float32)
    weighted_query = query * jnp.exp(cumul) * inherit[:, None, None] * scale
    local_gradient = jnp.einsum(
        "zie,zir->ier", weighted_query, mixed_gradient, precision=HIGH_PRECISION
    )
    through_all = jnp.exp(cumul[-1]) * (last_seg[0] == prior).astype(jnp.float32)
    nothing = jnp.zeros((), jnp.float32)
    outgoing, _ = chain(through_all[0], local_gradient[0], nothing, nothing, True, 8)
    d_query, d_key, d_value, d_logdec = mixer_back((mixed_gradient, outgoing))
    query_bf = d_query.reshape(length, local_heads * DK).astype(jnp.bfloat16)
    key_bf = d_key.reshape(length, local_heads * DK).astype(jnp.bfloat16)
    value_bf = d_value.reshape(length, local_heads * DV).astype(jnp.bfloat16)
    d_logit = d_logdec.reshape(length, local_heads * DK) * jax.nn.sigmoid(-logit) / 16.0
    grad_bias = jnp.sum(d_logit, axis=0).reshape(local_heads, DK)
    grad_rank = jnp.dot(low.T, d_logit, precision=HIGH_PRECISION).reshape(
        GATE_RANK, local_heads, DK
    )
    d_low = (
        jnp.einsum(
            "thk,rhk->thr",
            d_logit.reshape(length, local_heads, DK),
            rank_w.astype(jnp.float32).reshape(GATE_RANK, local_heads, DK),
            precision=HIGH_PRECISION,
        )
        .astype(jnp.bfloat16)
        .reshape(length, local_heads * GATE_RANK)
    )
    part_low = (
        jnp.dot(normed_in.T, d_low, preferred_element_type=jnp.float32)
        .reshape(D, local_heads, GATE_RANK)
        .sum(axis=1)
    )
    d_project = jnp.concatenate([query_bf, key_bf, value_bf, d_outgate], axis=1)
    grad_project = jnp.dot(normed_in.T, d_project, preferred_element_type=jnp.float32)
    low_rows = low_w.T
    total_term = jnp.dot(d_project, project_w.T, preferred_element_type=jnp.float32)
    d_normin = scatter_sum(
        (total_term + jnp.dot(d_low, low_rows, preferred_element_type=jnp.float32)).astype(
            jnp.bfloat16
        ),
        "head",
        9,
    )
    part_attn_gain = jnp.sum(d_normin * resid_in * inv_attn, axis=0)
    scaled_in = gain_attn * d_normin
    grad_in = (
        d_mid
        + inv_attn * scaled_in
        - resid_in * inv_attn**3 * jnp.mean(scaled_in * resid_in, axis=-1, keepdims=True)
    )

    def block(a):
        a = a.reshape(n, 1, -1)
        return jnp.pad(a, ((0, 0), (0, 0), (0, LANE - a.shape[2])))

    ranks = grad_rank[:, 0, :].reshape(GATE_RANK, n, DK // n).transpose(1, 0, 2)
    ranks = jnp.pad(
        ranks, ((0, 0), (0, rows - GATE_RANK), (0, spare - DK // n))
    ).astype(jnp.bfloat16)
    sums = jnp.concatenate(
        [block(part_attn_gain), block(part_mlp_gain), block(part_head_gain), block(grad_bias)],
        axis=1,
    )
    sums = jnp.pad(sums, ((0, 0), (0, rows - 4), (0, 0))).astype(jnp.bfloat16)
    grads = [
        g.astype(jnp.bfloat16).reshape(n, rows, -1)
        for g in (
            grad_project,
            grad_out,
            grad_gu,
        )
    ]
    grads.append(
        jnp.concatenate(
            [
                grad_down.astype(jnp.bfloat16).reshape(n, rows, wide),
                part_low.astype(jnp.bfloat16).reshape(n, rows, GATE_RANK),
                ranks,
                sums,
            ],
            axis=2,
        )
    )
    middle = (wide // LANE + 2) * LANE
    plan = (
        (2, 0, 0, middle),
        (3, 1, 0, grads[3].shape[2]),
        (0, 0, 0, edge_out),
        (2, 1, middle, 2 * wide - middle),
        (1, 1, 0, DV),
    )
    own_project, own_out, own_gu, own_rest = ring_sum(grads, plan, "shard", 10)
    heads = lax.axis_size("head")
    gain_rows = DV // n
    edge_lines = wide + GATE_RANK + spare
    final_rank = own_rest[:GATE_RANK, wide + GATE_RANK : wide + GATE_RANK + DK // n]
    final_bias = own_rest[3, edge_lines : edge_lines + DK // n]

    def owned_by(row, size):
        a = own_rest[row, edge_lines : edge_lines + size].reshape(heads, 1, size // heads)
        return jnp.pad(a, ((0, 0), (0, 0), (0, LANE - size // heads)))

    shares = jnp.concatenate([owned_by(0, rows), owned_by(1, rows), owned_by(2, gain_rows)], axis=1)
    low_share = own_rest[:, wide : wide + GATE_RANK].reshape(heads, rows // heads, GATE_RANK)
    low_share = jnp.pad(low_share, ((0, 0), (0, 0), (0, LANE - GATE_RANK)))
    shares = jnp.concatenate([low_share, shares], axis=1)
    deep = -(-(rows // heads + 3) // 32) * 32
    shares = jnp.pad(shares, ((0, 0), (0, deep - shares.shape[1]), (0, 0)))
    final = scatter_sum(shares.reshape(heads * deep, LANE).astype(jnp.bfloat16), "head", 11)
    low_rows = rows // heads
    return (
        resid_out,
        grad_in,
        final[low_rows, :low_rows],
        own_project[:, :DK],
        own_project[:, DK : 2 * DK],
        own_project[:, 2 * DK : 2 * DK + DV],
        own_project[:, 2 * DK + DV :],
        final[:low_rows, :GATE_RANK],
        final_rank.reshape(GATE_RANK, 1, DK // n),
        final_bias.reshape(1, DK // n),
        final[low_rows + 2, : gain_rows // heads],
        own_out.T,
        final[low_rows + 1, :low_rows],
        own_gu[:, :wide],
        own_gu[:, wide:],
        own_rest[:, :wide].T,
    )


def solution(mesh):
    in_specs = (
        P(("shard", "head"), None),
        P(("shard", "head"), None),
        P("shard"),
        P("shard"),
        P("shard", "head"),
        P("shard", "head"),
        P("shard", "head"),
        P("shard", "head"),
        P("shard", None),
        P(None, "head", "shard"),
        P("head", "shard"),
        P("shard"),
        P("head", "shard"),
        P("shard"),
        P("shard", "head"),
        P("shard", "head"),
        P("head", "shard"),
    )
    out_specs = (
        P(("shard", "head"), None),
        P(("shard", "head"), None),
        P(("shard", "head")),
        P("shard", "head"),
        P("shard", "head"),
        P("shard", "head"),
        P("shard", "head"),
        P(("shard", "head"), None),
        P(None, "head", "shard"),
        P("head", "shard"),
        P(("shard", "head")),
        P("head", "shard"),
        P(("shard", "head")),
        P("shard", "head"),
        P("shard", "head"),
        P("head", "shard"),
    )
    return jax.shard_map(
        on_device, mesh=mesh, in_specs=in_specs, out_specs=out_specs, check_vma=False
    )
```
